128 devices in a mesh: ctx: 32 (over y, x, z_hi), ch: 4 (over z_lo, core).
Axes of the slice: x: 4, y: 4, z: 4 (z_hi: 2, z_lo: 2; z = z_hi * 2 + z_lo), core: 2. Of those that a mesh axis runs over, the one named last changes fastest.
Arguments:
- grad_out: bfloat16 [32, 2, 256, 4096], P('ctx', None, None, 'ch'), may hold values from -6 to 6
- out_weight: bfloat16 [4096, 4096], P('ch'), may hold values from -0.09375 to 0.09375
- gate: bfloat16 [32, 2, 256, 4096], P('ctx', None, None, 'ch'), may hold values from -6 to 6
- filter_taps: float32 [768, 4096], P(None, 'ch'), may hold values from -0.21875 to 0.21875
- doc_starts: int32 [128], replicated, may hold values from 0 to 16384, as said below
Outputs:
- grad_input: float32 [32, 2, 256, 4096], P('ctx', None, None, 'ch')
The draws below stay inside these ranges and needn't reach their ends.
Inputs may be any that keep to these rules, and one draw needn't show every extreme that they name: `doc_starts`: Non-decreasing; the first is 0; offsets below 16384 start documents, the others equal 16384. Every document is at most 768 tokens long and every one but the last at least 128; one has exactly 768 tokens and one exactly 128.
All inputs are finite; a program needn't handle non-finite values.
Results may differ from the reference program's by a relative error of at most 0.0029.
Values may be sent and summed in bfloat16 or wider, within the bound.
A program may use at most 192 MiB of HBM per device.

```python
import jax
import jax.numpy as jnp
from jax import lax

C = 4096
CL = 256
REACH = 3
PAIRS = 32
NCH = 64
SEQ = 16384
N2 = 512
FL = 768
NDOC = 128


def draw_doc_starts(key, part):
    gap_key, first_key, second_key = jax.random.split(key, 3)
    gaps = jax.random.randint(gap_key, (NDOC,), CL // 2, FL + 1)
    longest = jax.random.randint(first_key, (), 0, 2)
    shortest = longest + 1 + jax.random.randint(second_key, (), 0, 2)
    order = jnp.arange(NDOC)
    gaps = jnp.where(order == longest, FL, gaps)
    gaps = jnp.where(order == shortest, CL // 2, gaps)
    starts = jnp.concatenate([jnp.zeros((1,), jnp.int32), jnp.cumsum(gaps)[:-1].astype(jnp.int32)])
    return jnp.minimum(starts, SEQ).astype(jnp.int32)


def levels(key, dims, pieces, smallest, largest):
    factor_of = 1.0
    for axis_at, shards_of in pieces:
        draws = jax.random.uniform(jax.random.fold_in(jax.random.fold_in(key, 6), axis_at), (shards_of,), jnp.float32, smallest / len(pieces), largest / len(pieces))
        factor_of = factor_of * jnp.repeat(jnp.exp(draws), dims[axis_at] // shards_of).reshape((-1,) + (1,) * (len(dims) - 1 - axis_at))
    return factor_of


def normal_values(key, dims, width, limit, pieces=(), kind=jnp.bfloat16):
    values = width * jax.random.normal(key, dims, jnp.float32)
    if pieces:
        values = values * levels(key, dims, pieces, -0.22, 0.18)
    return jnp.clip(values, -limit, limit).astype(kind)


def setup_inputs(seed: int = 0) -> dict:
    seeds = jax.random.split(jax.random.key(seed), 6)
    grad_out = normal_values(seeds[0], (PAIRS, 2, CL, C), 1.0, 6.0, ((0, 32), (3, 4)))
    out_weight = normal_values(seeds[1], (C, C), C ** -0.5, 0.09375, ((0, 4),))
    gate = normal_values(seeds[2], (PAIRS, 2, CL, C), 1.0, 6.0, ((0, 32), (3, 4)))
    filter_taps = normal_values(seeds[3], (FL, C), FL ** -0.5, 0.21875, ((1, 4),), jnp.float32)
    doc_starts = draw_doc_starts(jax.random.fold_in(seeds[5], 71), 0)
    return {"grad_out": grad_out, "out_weight": out_weight, "gate": gate, "filter_taps": filter_taps, "doc_starts": doc_starts}


def to_bfloat(values):
    return lax.optimization_barrier(values.astype(jnp.bfloat16)).astype(jnp.float32)


def unfold(folded):
    return jnp.concatenate([folded[:, 0], folded[::-1, 1]], axis=0)


def fold(blocks):
    return jnp.stack([blocks[:PAIRS], blocks[PAIRS:][::-1]], axis=1)


def reference(grad_out, out_weight, gate, filter_taps, doc_starts):
    rows = grad_out.reshape(-1, C)
    projected = jnp.dot(rows, out_weight.T, preferred_element_type=jnp.float32).reshape(grad_out.shape)
    conv_grad = to_bfloat(projected * gate.astype(jnp.float32))
    blocks = unfold(conv_grad)
    positions = jnp.arange(SEQ, dtype=jnp.int32)
    doc_index = jnp.sum((doc_starts[None, :] <= positions[:, None]).astype(jnp.int32), axis=1) - 1
    doc_index = doc_index.reshape(NCH, CL)
    first_doc = doc_index[:, 0]
    last_doc = doc_index[:, -1]
    segment = doc_index - first_doc[:, None]
    taps = filter_taps.astype(jnp.float32)
    offsets = jnp.arange(N2, dtype=jnp.int32)

    def kernel_spectrum(distance):
        lag = jnp.where(offsets < CL, distance * CL - offsets, distance * CL + N2 - offsets)
        valid = (lag >= 0) & (lag < FL)
        kernel = jnp.where(valid[:, None], taps[jnp.clip(lag, 0, FL - 1)], 0.0)
        return jnp.fft.rfft(kernel, axis=0)

    def spectrum(values):
        padded = jnp.concatenate([values, jnp.zeros_like(values)], axis=1)
        return jnp.fft.rfft(padded, axis=1)

    def inverse(product):
        return jnp.fft.irfft(product, n=N2, axis=1)[:, :CL]

    result = jnp.zeros((NCH, CL, C), jnp.float32)
    base = kernel_spectrum(0)
    leading = None
    for part in range(3):
        mask = (segment == part)[:, :, None]
        masked = jnp.where(mask, blocks, 0.0)
        spec_part = spectrum(masked)
        if part == 0:
            leading = spec_part
        result = result + jnp.where(mask, inverse(base[None] * spec_part), 0.0)
    tail_mask = (doc_index == last_doc[:, None])[:, :, None]
    for distance in range(1, REACH + 1):
        later = jnp.concatenate([leading[distance:], jnp.zeros_like(leading[:distance])], axis=0)
        later_first = jnp.concatenate([first_doc[distance:], jnp.full((distance,), -1, jnp.int32)])
        joined = (later_first == last_doc)[:, None, None]
        term = inverse(kernel_spectrum(distance)[None] * later)
        result = result + jnp.where(joined & tail_mask, term, 0.0)
    return fold(result)
```

```python
import functools
import math

import jax
import jax.numpy as jnp
import ml_dtypes
import numpy as np
from jax import lax
from jax.experimental import pallas as pl
from jax.experimental.pallas import tpu as pltpu
from jax.sharding import PartitionSpec as P

MESH = pl.DeviceIdType.MESH
BF = jnp.bfloat16
F32 = jnp.float32

CHUNKS = 2
TILE = 256
OWN_L, OWN_U, LX, LZ, LF, UX, UZ, UF = range(8)
S_LX, S_LZ, S_LF, S_UX, S_UZ, S_UF, S_TURN = range(7)


def dft_tables(block):
    order = np.concatenate([np.arange(0, block, 2), np.arange(1, block, 2)])
    omega = 2.0 * math.pi * (order + 0.5) / (2 * block)
    angle = omega[:, None] * np.arange(block)[None, :]
    forward = np.concatenate([np.cos(angle), -np.sin(angle)], axis=0)

    def parts(table):
        high = table.astype(ml_dtypes.bfloat16)
        low = (table - high.astype(np.float64)).astype(ml_dtypes.bfloat16)
        return high, low

    high, low = parts(forward)
    fwd = np.concatenate([high, low, high], axis=1)
    high, low = parts(forward.T / block)
    back = np.concatenate([high, low, high], axis=1)
    return fwd, back


def kernel(
    sizes,
    g_hbm, w_hbm, gate_hbm, taps_hbm, starts_ref, fwd_hbm, back_hbm,
    out_hbm,
    gath, wbuf, gate, taps, fwd, back, pacc, slots, kern, tot, early, masks,
    load_sem, out_sem, ag_send, ag_recv, halo_send, halo_recv,
):
    pairs, block, width, seq = sizes
    n_slots = 4
    rows = 2 * block
    rc = block // CHUNKS
    n_ag = 2 * CHUNKS
    tiles = width // TILE
    last_m = pairs // 2 - 1

    p = lax.axis_index("ctx")
    h = lax.axis_index("ch")
    m = p // 2
    zh = p % 2
    sib_h = h + 1 - 2 * (h % 2)
    zp_h = (h + 2) % 4
    zps_h = (sib_h + 2) % 4
    sib = (p, sib_h)
    zp = (p, zp_h)
    zx = (p + 1 - 2 * zh, h)
    xm = ((p + pairs - 2) % pairs, h)
    xp = ((p + 2) % pairs, h)
    at_turn = m == last_m
    is_last = p == pairs - 1

    loads = [
        pltpu.make_async_copy(fwd_hbm, fwd, load_sem.at[0]),
        pltpu.make_async_copy(taps_hbm, taps, load_sem.at[1]),
        pltpu.make_async_copy(back_hbm, back, load_sem.at[2]),
        pltpu.make_async_copy(gate_hbm, gate, load_sem.at[3]),
        pltpu.make_async_copy(g_hbm, gath.at[:, pl.ds(0, width)], load_sem.at[4]),
    ]
    for i, owner in enumerate((h, sib_h, zp_h, zps_h)):
        loads.append(
            pltpu.make_async_copy(
                w_hbm.at[:, pl.ds(pl.multiple_of(owner * width, width), width)],
                wbuf.at[:, pl.ds(i * width, width)],
                load_sem.at[5 + i],
            )
        )

    barrier = pltpu.get_barrier_semaphore()
    for peer in (sib, zp, zx, xm, xp):
        pl.semaphore_signal(barrier, inc=1, device_id=peer, device_id_type=MESH)
    for cp in loads[:2]:
        cp.start()
    pl.semaphore_wait(barrier, 5)

    def ag_z(k):
        r = pl.ds(k * rc, rc)
        return pltpu.make_async_remote_copy(
            src_ref=g_hbm.at[r],
            dst_ref=gath.at[r, pl.ds(2 * width, width)],
            send_sem=ag_send.at[k],
            recv_sem=ag_recv.at[k],
            device_id=zp,
            device_id_type=MESH,
        )

    def ag_f(k):
        r = pl.ds(k * rc, rc)
        return pltpu.make_async_remote_copy(
            src_ref=gath.at[r, pl.ds(2 * width, width)],
            dst_ref=gath.at[r, pl.ds(3 * width, width)],
            send_sem=ag_send.at[n_ag + k],
            recv_sem=ag_recv.at[n_ag + k],
            device_id=sib,
            device_id_type=MESH,
        )

    ag_s = pltpu.make_async_remote_copy(
        src_ref=g_hbm,
        dst_ref=gath.at[:, pl.ds(width, width)],
        send_sem=ag_send.at[2 * n_ag],
        recv_sem=ag_recv.at[2 * n_ag],
        device_id=sib,
        device_id_type=MESH,
    )
    for k in range(n_ag):
        ag_z(k).start()
    ag_s.start()
    for cp in loads[2:]:
        cp.start()

    def halo(kind, c, src, dst, dev, recv_kind=None):
        r = pl.ds(c * rc, rc)
        return pltpu.make_async_remote_copy(
            src_ref=slots.at[src, r],
            dst_ref=slots.at[dst, r],
            send_sem=halo_send.at[kind, c],
            recv_sem=halo_recv.at[kind if recv_kind is None else recv_kind, c],
            device_id=dev,
            device_id_type=MESH,
        )

    lz_src = jnp.where(zh == 1, OWN_L, LX)
    uz_src = jnp.where(zh == 0, OWN_U, UX)
    lf_src = jnp.where(is_last, OWN_U, LZ)

    def send_lx(c):
        return halo(S_LX, c, OWN_L, LX, xm)

    def send_turn(c):
        return halo(S_TURN, c, OWN_U, LX, zx, S_LX)

    def send_lz(c):
        return halo(S_LZ, c, lz_src, LZ, zx)

    def send_lf(c):
        return halo(S_LF, c, lf_src, LF, xm)

    def send_ux(c):
        return halo(S_UX, c, OWN_U, UX, xp)

    def send_uz(c):
        return halo(S_UZ, c, uz_src, UZ, zx)

    def send_uf(c):
        return halo(S_UF, c, UZ, UF, xp)

    has_lx = jnp.logical_not(is_last)
    does_lx = m > 0
    does_lz = jnp.logical_or(zh == 1, m < last_m)
    has_lz = jnp.logical_or(zh == 0, m < last_m)
    does_lf = m > 0
    has_lf = m < last_m
    does_ux = m < last_m
    has_ux = m > 0
    does_uz = jnp.logical_or(zh == 0, m > 0)
    has_uz = jnp.logical_or(zh == 1, m > 0)
    does_uf = jnp.logical_and(m < last_m, p > 0)
    has_uf = jnp.logical_and(m > 0, p > 2)

    starts = starts_ref[...]

    def doc_rows(base):
        pos = base + lax.broadcasted_iota(jnp.int32, (block, 128), 0)
        return jnp.sum((starts <= pos).astype(F32), axis=1, keepdims=True), pos[:, :1]

    def doc_at(pos):
        return jnp.sum((starts <= pos).astype(F32), axis=1, keepdims=True)

    def put_mask(i, cond):
        masks[i] = jnp.broadcast_to(jnp.where(cond, 1.0, 0.0), (block, TILE)).astype(BF)

    for b in range(2):
        k = p if b == 0 else 2 * pairs - 1 - p
        base = k * block
        first = doc_at(base)
        last = doc_at(base + block - 1)
        own, _ = doc_rows(base)
        put_mask(b * 6 + 0, own == last)
        put_mask(b * 6 + 4, jnp.logical_and(own == first, own != last))
        put_mask(b * 6 + 5, jnp.logical_and(own == first + 1, own != last))
        for d in range(1, 4):
            later, pos = doc_rows(base + d * block)
            put_mask(b * 6 + d, jnp.logical_and(later == last, pos < seq))

    for cp in loads[:2]:
        cp.wait()
    half = block // 2

    def taps_body(t, carry):
        cols = pl.ds(pl.multiple_of(t * TILE, TILE), TILE)
        prev = None
        for b in range(4):
            if b < 3:
                tap = taps[pl.ds(b * block, block), cols]
                high = tap.astype(BF)
                low = (tap - high.astype(F32)).astype(BF)
                spec = jnp.dot(
                    fwd[...],
                    jnp.concatenate([high, high, low], axis=0),
                    preferred_element_type=F32,
                )
                re, im = spec[:block], -spec[block:]
            else:
                re, im = None, None
            if prev is None:
                kre, kim = re, im
            else:
                pre, pim = prev
                turn_re = jnp.concatenate([pim[:half], -pim[half:]], axis=0)
                turn_im = jnp.concatenate([-pre[:half], pre[half:]], axis=0)
                if re is None:
                    kre, kim = turn_re, turn_im
                else:
                    kre, kim = re + turn_re, im + turn_im
            kern[b, pl.ds(0, block), cols] = kre
            kern[b, pl.ds(block, block), cols] = kim
            prev = (re, im)
        return carry

    lax.fori_loop(0, tiles, taps_body, 0)

    loads[4].wait()
    loads[5].wait()
    loads[6].wait()
    ag_s.wait_recv()
    nt = (((1,), (1,)), ((), ()))

    def base_body(t, carry):
        cols = pl.ds(pl.multiple_of(t * TILE, TILE), TILE)
        pacc[:, cols] = lax.dot_general(
            gath[:, pl.ds(0, 2 * width)],
            wbuf[cols, pl.ds(0, 2 * width)],
            nt,
            preferred_element_type=F32,
        )
        return carry

    lax.fori_loop(0, tiles, base_body, 0)

    def project(k):
        b, c = divmod(k, CHUNKS)
        r = pl.ds(k * rc, rc)

        def body(t, carry):
            cols = pl.ds(pl.multiple_of(t * TILE, TILE), TILE)
            part = lax.dot_general(
                gath[r, pl.ds(2 * width, 2 * width)],
                wbuf[cols, pl.ds(2 * width, 2 * width)],
                nt,
                preferred_element_type=F32,
            )
            value = (pacc[r, cols] + part) * gate[r, cols].astype(F32)
            slots[b, pl.ds(c * rc, rc), cols] = value.astype(BF)
            return carry

        lax.fori_loop(0, tiles, body, 0)

    def spectrum(x, mask):
        xm_ = x * mask
        spec = jnp.dot(
            fwd[:, pl.ds(0, 2 * block)],
            jnp.concatenate([xm_, xm_], axis=0),
            preferred_element_type=F32,
        )
        return spec[:block], spec[block:]

    def inverse(tre, tim):
        total = jnp.concatenate([tre, tim], axis=0)
        high = total.astype(BF)
        low = (total - high.astype(F32)).astype(BF)
        return jnp.dot(
            back[...],
            jnp.concatenate([high, high, low], axis=0),
            preferred_element_type=F32,
        )

    def product(d, cols, re, im):
        kre = kern[d, pl.ds(0, block), cols]
        kim = kern[d, pl.ds(block, block), cols]
        return kre * re - kim * im, kre * im + kim * re

    def own_block(b):
        def body(t, carry):
            cols = pl.ds(pl.multiple_of(t * TILE, TILE), TILE)
            x = slots[b, :, cols]
            re, im = spectrum(x, masks[b * 6])
            tre, tim = product(0, cols, re, im)
            tot[b, pl.ds(0, block), cols] = tre
            tot[b, pl.ds(block, block), cols] = tim
            result = None
            for s in (4, 5):
                mask = masks[b * 6 + s]
                re, im = spectrum(x, mask)
                tre, tim = product(0, cols, re, im)
                part = inverse(tre, tim) * mask.astype(F32)
                result = part if result is None else result + part
            early[b, :, cols] = result
            return carry

        lax.fori_loop(0, tiles, body, 0)

    def cross(b, d, slot):
        def body(t, carry):
            cols = pl.ds(pl.multiple_of(t * TILE, TILE), TILE)
            re, im = spectrum(slots[slot, :, cols], masks[b * 6 + d])
            tre, tim = product(d, cols, re, im)
            tot[b, pl.ds(0, block), cols] += tre
            tot[b, pl.ds(block, block), cols] += tim
            return carry

        lax.fori_loop(0, tiles, body, 0)

    def finish(b):
        def body(t, carry):
            cols = pl.ds(pl.multiple_of(t * TILE, TILE), TILE)
            value = inverse(tot[b, pl.ds(0, block), cols], tot[b, pl.ds(block, block), cols])
            early[b, :, cols] += value * masks[b * 6].astype(F32)
            return carry

        lax.fori_loop(0, tiles, body, 0)

    def out_copy(b):
        return pltpu.make_async_copy(early.at[b], out_hbm.at[b], out_sem.at[b])

    def when(cond, fn):
        pl.when(cond)(fn)

    def gather_step(k):
        ag_z(k).wait_recv()
        ag_f(k).start()
        ag_f(k).wait_recv()
        project(k)

    loads[3].wait()
    loads[7].wait()
    loads[8].wait()
    for c in range(CHUNKS):
        gather_step(c)
        when(does_lx, lambda c=c: send_lx(c).start())
    loads[2].wait()
    own_block(0)

    for c in range(CHUNKS):
        gather_step(CHUNKS + c)
        when(does_ux, lambda c=c: send_ux(c).start())

    for c in range(CHUNKS):
        when(has_lx & jnp.logical_not(at_turn), lambda c=c: send_lx(c).wait_recv())
        when(does_lz, lambda c=c: send_lz(c).start())

    @pl.when(is_last)
    def _():
        for c in range(CHUNKS):
            send_turn(c).start()

    for c in range(CHUNKS):
        when(zh == 0, lambda c=c: send_uz(c).start())

    own_block(1)

    for c in range(CHUNKS):
        when(has_ux, lambda c=c: send_ux(c).wait_recv())
        when(jnp.logical_and(zh == 1, m > 0), lambda c=c: send_uz(c).start())

    cross(1, 2, jnp.where(m > 0, UX, OWN_U))
    when(jnp.logical_not(at_turn), lambda: cross(0, 2, LX))

    for c in range(CHUNKS):
        when(has_lz, lambda c=c: send_lz(c).wait_recv())
        when(does_lf, lambda c=c: send_lf(c).start())

    when(jnp.logical_not(at_turn), lambda: cross(0, 1, LZ))

    for c in range(CHUNKS):
        when(has_uz, lambda c=c: send_uz(c).wait_recv())
        when(does_uf, lambda c=c: send_uf(c).start())

    @pl.when(at_turn)
    def _():
        for c in range(CHUNKS):
            when(has_lx, lambda c=c: send_lx(c).wait_recv())
        cross(0, 1, jnp.where(zh == 1, OWN_U, LZ))
        cross(0, 2, jnp.where(zh == 1, UZ, LX))

    for c in range(CHUNKS):
        when(has_lf, lambda c=c: send_lf(c).wait_recv())
    cross(0, 3, jnp.where(at_turn, jnp.where(zh == 1, UX, OWN_U), LF))
    finish(0)
    out_copy(0).start()
    cross(1, 1, jnp.where(p > 0, UZ, OWN_U))
    for c in range(CHUNKS):
        when(has_uf, lambda c=c: send_uf(c).wait_recv())
    cross(1, 3, jnp.where(p > 2, UF, OWN_U))
    finish(1)
    out_copy(1).start()

    for k in range(n_ag):
        ag_z(k).wait_send()
        ag_f(k).wait_send()
    ag_s.wait_send()
    for c in range(CHUNKS):
        when(does_lx, lambda c=c: send_lx(c).wait_send())
        when(does_lz, lambda c=c: send_lz(c).wait_send())
        when(does_lf, lambda c=c: send_lf(c).wait_send())
        when(does_ux, lambda c=c: send_ux(c).wait_send())
        when(does_uz, lambda c=c: send_uz(c).wait_send())
        when(does_uf, lambda c=c: send_uf(c).wait_send())
        when(is_last, lambda c=c: send_turn(c).wait_send())
    out_copy(0).wait()
    out_copy(1).wait()


def on_device(grad_out, out_weight, gate, filter_taps, doc_starts):
    pairs = lax.axis_size("ctx")
    block = grad_out.shape[2]
    width = out_weight.shape[0]
    rows = 2 * block
    features = out_weight.shape[1]
    fwd, back = dft_tables(block)
    any_spec = pl.BlockSpec(memory_space=pl.ANY)
    call = pl.pallas_call(
        functools.partial(kernel, (pairs, block, width, 2 * pairs * block)),
        out_shape=jax.ShapeDtypeStruct((2, block, width), F32),
        in_specs=[
            any_spec, any_spec, any_spec, any_spec,
            pl.BlockSpec(memory_space=pltpu.VMEM),
            any_spec, any_spec,
        ],
        out_specs=any_spec,
        scratch_shapes=[
            pltpu.VMEM((rows, features), BF),
            pltpu.VMEM((width, features), BF),
            pltpu.VMEM((rows, width), BF),
            pltpu.VMEM(filter_taps.shape, F32),
            pltpu.VMEM(fwd.shape, BF),
            pltpu.VMEM(back.shape, BF),
            pltpu.VMEM((rows, width), F32),
            pltpu.VMEM((8, block, width), BF),
            pltpu.VMEM((4, 2 * block, width), F32),
            pltpu.VMEM((2, 2 * block, width), F32),
            pltpu.VMEM((2, block, width), F32),
            pltpu.VMEM((12, block, TILE), BF),
            pltpu.SemaphoreType.DMA((9,)),
            pltpu.SemaphoreType.DMA((2,)),
            pltpu.SemaphoreType.DMA((4 * CHUNKS + 1,)),
            pltpu.SemaphoreType.DMA((4 * CHUNKS + 1,)),
            pltpu.SemaphoreType.DMA((7, CHUNKS)),
            pltpu.SemaphoreType.DMA((6, CHUNKS)),
        ],
        compiler_params=pltpu.CompilerParams(
            collective_id=0, has_side_effects=True, vmem_limit_bytes=56 << 20
        ),
        name="gated_conv_grad",
    )
    result = call(
        grad_out.reshape(rows, width),
        out_weight,
        gate.reshape(rows, width),
        filter_taps,
        doc_starts.reshape(1, -1),
        jnp.asarray(fwd),
        jnp.asarray(back),
    )
    return result[None]


def solution(mesh):
    in_specs = (
        P("ctx", None, None, "ch"),
        P("ch", None),
        P("ctx", None, None, "ch"),
        P(None, "ch"),
        P(),
    )
    out_specs = P("ctx", None, None, "ch")
    return jax.shard_map(
        on_device, mesh=mesh, in_specs=in_specs, out_specs=out_specs, check_vma=False
    )
```

```python
import functools
import math

import jax
import jax.numpy as jnp
import ml_dtypes
import numpy as np
from jax import lax
from jax.experimental import pallas as pl
from jax.experimental.pallas import tpu as pltpu
from jax.sharding import PartitionSpec as P

MESH = pl.DeviceIdType.MESH
BF = jnp.bfloat16
F32 = jnp.float32

GATHER = 2
CHUNKS = 4
TILE = 256
OWN_L, OWN_U, LX, LZ, LF, UX, UZ, UF = range(8)
S_LX, S_LZ, S_LF, S_UX, S_UZ, S_UF = range(6)


def dft_tables(block):
    order = np.concatenate([np.arange(0, block, 2), np.arange(1, block, 2)])
    omega = 2.0 * math.pi * (order + 0.5) / (2 * block)
    angle = omega[:, None] * np.arange(block)[None, :]
    forward = np.concatenate([np.cos(angle), -np.sin(angle)], axis=0)

    def parts(table):
        high = table.astype(ml_dtypes.bfloat16)
        low = (table - high.astype(np.float64)).astype(ml_dtypes.bfloat16)
        return high, low

    high, low = parts(forward)
    fwd = np.concatenate([high, low, high], axis=1)
    high, low = parts(forward.T / block)
    back = np.concatenate([high, low, high], axis=1)
    return fwd, back


def kernel(
    sizes,
    g_hbm, w_hbm, gate_hbm, taps_hbm, starts_hbm, fwd_hbm, back_hbm,
    out,
    gath, wbuf, gate, taps, starts_ref, fwd, back, pacc, slots, kern, tot, masks,
    load_sem, ag_send, ag_recv, halo_send, halo_recv,
):
    pairs, block, width, seq = sizes
    ra = block // GATHER
    rc = block // CHUNKS
    n_ag = 2 * GATHER
    tiles = width // TILE
    last_m = pairs // 2 - 1

    p = lax.axis_index("ctx")
    h = lax.axis_index("ch")
    m = p // 2
    zh = p % 2
    sib_h = h + 1 - 2 * (h % 2)
    zp_h = (h + 2) % 4
    zps_h = (sib_h + 2) % 4
    sib = (p, sib_h)
    zp = (p, zp_h)
    zx = (p + 1 - 2 * zh, h)
    xm = ((p + pairs - 2) % pairs, h)
    xp = ((p + 2) % pairs, h)
    at_turn = m == last_m
    is_last = p == pairs - 1
    turned = p == pairs - 2

    loads = [
        pltpu.make_async_copy(fwd_hbm, fwd, load_sem.at[0]),
        pltpu.make_async_copy(taps_hbm, taps, load_sem.at[1]),
        pltpu.make_async_copy(back_hbm, back, load_sem.at[2]),
        pltpu.make_async_copy(gate_hbm, gate, load_sem.at[3]),
        pltpu.make_async_copy(g_hbm, gath.at[:, pl.ds(0, width)], load_sem.at[4]),
    ]
    for i, owner in enumerate((h, sib_h, zp_h, zps_h)):
        loads.append(
            pltpu.make_async_copy(
                w_hbm.at[:, pl.ds(pl.multiple_of(owner * width, width), width)],
                wbuf.at[:, pl.ds(i * width, width)],
                load_sem.at[5 + i],
            )
        )
    loads.append(pltpu.make_async_copy(starts_hbm, starts_ref, load_sem.at[9]))

    barrier = pltpu.get_barrier_semaphore()
    for peer in (sib, zp, zx, xm, xp):
        pl.semaphore_signal(barrier, inc=1, device_id=peer, device_id_type=MESH)
    for cp in loads[:2] + loads[9:]:
        cp.start()
    pl.semaphore_wait(barrier, 5)

    def ag_z(k):
        r = pl.ds(k * ra, ra)
        return pltpu.make_async_remote_copy(
            src_ref=g_hbm.at[r],
            dst_ref=gath.at[r, pl.ds(2 * width, width)],
            send_sem=ag_send.at[k],
            recv_sem=ag_recv.at[k],
            device_id=zp,
            device_id_type=MESH,
        )

    def ag_f(k):
        r = pl.ds(k * ra, ra)
        return pltpu.make_async_remote_copy(
            src_ref=gath.at[r, pl.ds(2 * width, width)],
            dst_ref=gath.at[r, pl.ds(3 * width, width)],
            send_sem=ag_send.at[n_ag + k],
            recv_sem=ag_recv.at[n_ag + k],
            device_id=sib,
            device_id_type=MESH,
        )

    ag_s = pltpu.make_async_remote_copy(
        src_ref=g_hbm,
        dst_ref=gath.at[:, pl.ds(width, width)],
        send_sem=ag_send.at[2 * n_ag],
        recv_sem=ag_recv.at[2 * n_ag],
        device_id=sib,
        device_id_type=MESH,
    )
    for k in range(n_ag):
        ag_z(k).start()
    ag_s.start()
    for cp in loads[2:9]:
        cp.start()

    def halo(kind, c, src, dst, dev, recv_kind=None):
        r = pl.ds(c * rc, rc)
        return pltpu.make_async_remote_copy(
            src_ref=slots.at[src, r],
            dst_ref=slots.at[dst, r],
            send_sem=halo_send.at[kind, c],
            recv_sem=halo_recv.at[kind if recv_kind is None else recv_kind, c],
            device_id=dev,
            device_id_type=MESH,
        )

    lz_src = jnp.where(zh == 1, OWN_L, LX)
    uz_src = jnp.where(zh == 0, OWN_U, UX)
    lf_src = jnp.where(is_last, OWN_U, LZ)
    lx_src = jnp.where(m > 0, OWN_L, UZ)

    def send_lx(c):
        return halo(S_LX, c, lx_src, LX, xm)

    def send_lz(c):
        return halo(S_LZ, c, lz_src, LZ, zx)

    def send_lf(c):
        return halo(S_LF, c, lf_src, LF, xm)

    def send_ux(c):
        return halo(S_UX, c, OWN_U, UX, xp)

    def send_uz(c):
        return halo(S_UZ, c, uz_src, UZ, zx)

    def send_uf(c):
        return halo(S_UF, c, UZ, UF, xp)

    does_lx = jnp.logical_or(m > 0, p == 0)
    does_lz = jnp.logical_or(zh == 1, m < last_m)
    has_lz = jnp.logical_or(zh == 0, m < last_m)
    does_lf = m > 0
    has_lf = m < last_m
    relays = p == 0
    does_ux = jnp.logical_or(m < last_m, is_last)
    has_ux = p > 0
    does_uf = jnp.logical_and(m < last_m, p > 0)
    has_uf = jnp.logical_and(m > 0, p > 2)

    loads[9].wait()
    starts = starts_ref[...]

    def doc_rows(base):
        pos = base + lax.broadcasted_iota(jnp.int32, (block, 128), 0)
        return jnp.sum((starts <= pos).astype(F32), axis=1, keepdims=True), pos[:, :1]

    def doc_at(pos):
        return jnp.sum((starts <= pos).astype(F32), axis=1, keepdims=True)

    def put_mask(i, cond):
        masks[i] = jnp.broadcast_to(jnp.where(cond, 1.0, 0.0), (block, TILE)).astype(BF)

    for b in range(2):
        k = p if b == 0 else 2 * pairs - 1 - p
        base = k * block
        first = doc_at(base)
        last = doc_at(base + block - 1)
        own, _ = doc_rows(base)
        put_mask(b * 6 + 0, own == last)
        put_mask(b * 6 + 4, jnp.logical_and(own == first, own != last))
        put_mask(b * 6 + 5, jnp.logical_and(own == first + 1, own != last))
        for d in range(1, 4):
            later, pos = doc_rows(base + d * block)
            put_mask(b * 6 + d, jnp.logical_and(later == last, pos < seq))

    for cp in loads[:2]:
        cp.wait()
    half = block // 2

    def taps_body(t, carry):
        cols = pl.ds(pl.multiple_of(t * TILE, TILE), TILE)
        prev = None
        for b in range(4):
            if b < 3:
                tap = taps[pl.ds(b * block, block), cols]
                high = tap.astype(BF)
                low = (tap - high.astype(F32)).astype(BF)
                spec = jnp.dot(
                    fwd[...],
                    jnp.concatenate([high, high, low], axis=0),
                    preferred_element_type=F32,
                )
                re, im = spec[:block], -spec[block:]
            else:
                re, im = None, None
            if prev is None:
                kre, kim = re, im
            else:
                pre, pim = prev
                turn_re = jnp.concatenate([pim[:half], -pim[half:]], axis=0)
                turn_im = jnp.concatenate([-pre[:half], pre[half:]], axis=0)
                if re is None:
                    kre, kim = turn_re, turn_im
                else:
                    kre, kim = re + turn_re, im + turn_im
            kern[b, pl.ds(0, block), cols] = kre
            kern[b, pl.ds(block, block), cols] = kim
            prev = (re, im)
        return carry

    lax.fori_loop(0, tiles, taps_body, 0)

    loads[4].wait()
    loads[5].wait()
    loads[6].wait()
    ag_s.wait_recv()
    nt = (((1,), (1,)), ((), ()))

    def base_body(t, carry):
        cols = pl.ds(pl.multiple_of(t * TILE, TILE), TILE)
        pacc[:, cols] = lax.dot_general(
            gath[:, pl.ds(0, 2 * width)],
            wbuf[cols, pl.ds(0, 2 * width)],
            nt,
            preferred_element_type=F32,
        )
        return carry

    lax.fori_loop(0, tiles, base_body, 0)

    def project(k):
        b, c = divmod(k, GATHER)
        r = pl.ds(k * ra, ra)

        def body(t, carry):
            cols = pl.ds(pl.multiple_of(t * TILE, TILE), TILE)
            part = lax.dot_general(
                gath[r, pl.ds(2 * width, 2 * width)],
                wbuf[cols, pl.ds(2 * width, 2 * width)],
                nt,
                preferred_element_type=F32,
            )
            value = (pacc[r, cols] + part) * gate[r, cols].astype(F32)
            slots[b, pl.ds(c * ra, ra), cols] = value.astype(BF)
            return carry

        lax.fori_loop(0, tiles, body, 0)

    def spectrum(x, mask, first=0):
        n = x.shape[0]
        xm_ = x * mask
        if n == block:
            table = fwd[:, pl.ds(0, 2 * block)]
        else:
            table = jnp.concatenate(
                [fwd[:, pl.ds(first, n)], fwd[:, pl.ds(block + first, n)]], axis=1
            )
        spec = jnp.dot(
            table, jnp.concatenate([xm_, xm_], axis=0), preferred_element_type=F32
        )
        return spec[:block], spec[block:]

    def inverse(tre, tim):
        total = jnp.concatenate([tre, tim], axis=0)
        high = total.astype(BF)
        low = (total - high.astype(F32)).astype(BF)
        return jnp.dot(
            back[...],
            jnp.concatenate([high, high, low], axis=0),
            preferred_element_type=F32,
        )

    def product(d, cols, re, im):
        kre = kern[d, pl.ds(0, block), cols]
        kim = kern[d, pl.ds(block, block), cols]
        return kre * re - kim * im, kre * im + kim * re

    def own_tile(b, t):
        cols = pl.ds(t * TILE, TILE)
        x = slots[b, :, cols]
        re, im = spectrum(x, masks[b * 6])
        tre, tim = product(0, cols, re, im)
        tot[b, pl.ds(0, block), cols] = tre
        tot[b, pl.ds(block, block), cols] = tim
        result = None
        for s in (4, 5):
            mask = masks[b * 6 + s]
            re, im = spectrum(x, mask)
            tre, tim = product(0, cols, re, im)
            part = inverse(tre, tim) * mask.astype(F32)
            result = part if result is None else result + part
        out[b, :, cols] = result

    def cross(b, d, slot, first=0, count=None):
        n = block if count is None else count
        r = pl.ds(first, n)
        for t in range(tiles):
            cols = pl.ds(t * TILE, TILE)
            re, im = spectrum(slots[slot, r, cols], masks[b * 6 + d, r], first)
            tre, tim = product(d, cols, re, im)
            tot[b, pl.ds(0, block), cols] += tre
            tot[b, pl.ds(block, block), cols] += tim

    def finish(b):
        for t in range(tiles):
            cols = pl.ds(t * TILE, TILE)
            value = inverse(tot[b, pl.ds(0, block), cols], tot[b, pl.ds(block, block), cols])
            out[b, :, cols] += value * masks[b * 6].astype(F32)

    def when(cond, fn):
        pl.when(cond)(fn)

    def gather_step(k):
        ag_z(k).wait_recv()
        ag_f(k).start()
        ag_f(k).wait_recv()
        project(k)

    per = CHUNKS // GATHER

    def ux_to_uz(c):
        when(has_ux, lambda: send_ux(c).wait_recv())
        when(zh == 1, lambda: send_uz(c).start())

    def lz_to_lf(c):
        when(has_lz, lambda: send_lz(c).wait_recv())
        when(does_lf, lambda: send_lf(c).start())

    def uz_to_uf(c):
        send_uz(c).wait_recv()
        when(does_uf, lambda: send_uf(c).start())
        when(relays, lambda: send_lx(c).start())

    loads[3].wait()
    loads[7].wait()
    loads[8].wait()
    for k in range(GATHER):
        gather_step(k)
        for c in range(k * per, (k + 1) * per):
            when(m > 0, lambda c=c: send_lx(c).start())
    loads[2].wait()
    for t in range(tiles):
        own_tile(0, t)

    for k in range(GATHER):
        gather_step(GATHER + k)
        for c in range(k * per, (k + 1) * per):
            when(does_ux, lambda c=c: send_ux(c).start())
        if k == GATHER - 2:
            for c in range(CHUNKS):
                when(jnp.logical_not(at_turn), lambda c=c: send_lx(c).wait_recv())
                when(does_lz, lambda c=c: send_lz(c).start())
    for c in range(CHUNKS):
        when(zh == 0, lambda c=c: send_uz(c).start())

    when(jnp.logical_not(at_turn), lambda: cross(0, 2, LX))
    ux_to_uz(0)
    ux_to_uz(1)
    lz_to_lf(0)
    own_tile(1, 0)
    lz_to_lf(1)
    own_tile(1, 1)
    ux_to_uz(2)
    lz_to_lf(2)
    own_tile(1, 2)
    ux_to_uz(3)
    lz_to_lf(3)
    own_tile(1, 3)
    cross(0, 1, jnp.where(is_last, OWN_U, LZ))
    uz_to_uf(0)
    cross(1, 2, jnp.where(m > 0, UX, OWN_U))
    uz_to_uf(1)
    for c in range(CHUNKS):
        when(has_lf, lambda c=c: send_lf(c).wait_recv())
    cross(0, 3, jnp.where(at_turn, jnp.where(zh == 1, UX, OWN_U), LF))
    uz_to_uf(2)
    when(jnp.logical_not(at_turn), lambda: finish(0))
    uz_to_uf(3)
    cross(1, 1, jnp.where(p > 0, UZ, OWN_U))

    @pl.when(is_last)
    def _():
        cross(0, 2, UZ)
        finish(0)

    for j in range(2):
        for c in range(2 * j, 2 * j + 2):
            when(has_uf, lambda c=c: send_uf(c).wait_recv())
        cross(1, 3, jnp.where(p > 2, UF, OWN_U), j * (block // 2), block // 2)
    finish(1)

    @pl.when(turned)
    def _():
        for c in range(CHUNKS):
            send_lx(c).wait_recv()
        cross(0, 2, LX)
        finish(0)

    for k in range(n_ag):
        ag_z(k).wait_send()
        ag_f(k).wait_send()
    ag_s.wait_send()
    for c in range(CHUNKS):
        when(does_lx, lambda c=c: send_lx(c).wait_send())
        when(does_lz, lambda c=c: send_lz(c).wait_send())
        when(does_lf, lambda c=c: send_lf(c).wait_send())
        when(does_ux, lambda c=c: send_ux(c).wait_send())
        send_uz(c).wait_send()
        when(does_uf, lambda c=c: send_uf(c).wait_send())


def on_device(grad_out, out_weight, gate, filter_taps, doc_starts):
    pairs = lax.axis_size("ctx")
    block = grad_out.shape[2]
    width = out_weight.shape[0]
    rows = 2 * block
    features = out_weight.shape[1]
    fwd, back = dft_tables(block)
    hbm = pl.BlockSpec(memory_space=pltpu.HBM)
    call = pl.pallas_call(
        functools.partial(kernel, (pairs, block, width, 2 * pairs * block)),
        out_shape=jax.ShapeDtypeStruct((2, block, width), F32),
        in_specs=[hbm] * 7,
        out_specs=pl.BlockSpec(memory_space=pltpu.VMEM),
        scratch_shapes=[
            pltpu.VMEM((rows, features), BF),
            pltpu.VMEM((width, features), BF),
            pltpu.VMEM((rows, width), BF),
            pltpu.VMEM(filter_taps.shape, F32),
            pltpu.VMEM((1, doc_starts.shape[0]), jnp.int32),
            pltpu.VMEM(fwd.shape, BF),
            pltpu.VMEM(back.shape, BF),
            pltpu.VMEM((rows, width), F32),
            pltpu.VMEM((8, block, width), BF),
            pltpu.VMEM((4, 2 * block, width), F32),
            pltpu.VMEM((2, 2 * block, width), F32),
            pltpu.VMEM((12, block, TILE), BF),
            pltpu.SemaphoreType.DMA((10,)),
            pltpu.SemaphoreType.DMA((4 * GATHER + 1,)),
            pltpu.SemaphoreType.DMA((4 * GATHER + 1,)),
            pltpu.SemaphoreType.DMA((6, CHUNKS)),
            pltpu.SemaphoreType.DMA((6, CHUNKS)),
        ],
        compiler_params=pltpu.CompilerParams(
            collective_id=0, has_side_effects=True, vmem_limit_bytes=44 << 20
        ),
        name="gated_conv_grad",
    )
    operands = (
        grad_out.reshape(rows, width),
        out_weight,
        gate.reshape(rows, width),
        filter_taps,
        doc_starts.reshape(1, -1),
        jnp.asarray(fwd),
        jnp.asarray(back),
    )
    result = call(*[pltpu.with_memory_space_constraint(v, pltpu.HBM) for v in operands])
    return result[None]


def solution(mesh):
    in_specs = (
        P("ctx", None, None, "ch"),
        P("ch", None),
        P("ctx", None, None, "ch"),
        P(None, "ch"),
        P(),
    )
    out_specs = P("ctx", None, None, "ch")
    return jax.shard_map(
        on_device, mesh=mesh, in_specs=in_specs, out_specs=out_specs, check_vma=False
    )
```

```python
import functools
import math

import jax
import jax.numpy as jnp
import ml_dtypes
import numpy as np
from jax import lax
from jax.experimental import pallas as pl
from jax.experimental.pallas import tpu as pltpu
from jax.sharding import PartitionSpec as P

MESH = pl.DeviceIdType.MESH
BF = jnp.bfloat16
F32 = jnp.float32

GATHER = 2
PIECES = ((0, 64), (64, 64), (128, 64), (192, 32), (224, 32))
CHUNKS = len(PIECES)
TILE = 256
OWN_L, OWN_U, LX, LZ, LF, UX, UZ, UF = range(8)
S_LX, S_LZ, S_LF, S_UX, S_UZ, S_UF = range(6)


def dft_tables(block):
    order = np.concatenate([np.arange(0, block, 2), np.arange(1, block, 2)])
    omega = 2.0 * math.pi * (order + 0.5) / (2 * block)
    angle = omega[:, None] * np.arange(block)[None, :]
    forward = np.concatenate([np.cos(angle), -np.sin(angle)], axis=0)

    def parts(table):
        high = table.astype(ml_dtypes.bfloat16)
        low = (table - high.astype(np.float64)).astype(ml_dtypes.bfloat16)
        return high, low

    high, low = parts(forward)
    fwd = np.concatenate([high, low, high], axis=1)
    high, low = parts(forward.T / block)
    back = np.concatenate([high, low, high], axis=1)
    return fwd, back


def kernel(
    sizes,
    g_hbm, w_hbm, gate_hbm, taps_hbm, starts_hbm, fwd_hbm, back_hbm,
    out,
    gath, wbuf, gate, taps, starts_ref, fwd, back, pacc, slots, kern, tot, masks,
    load_sem, ag_send, ag_recv, halo_send, halo_recv,
):
    pairs, block, width, seq = sizes
    ra = block // GATHER
    n_ag = 2 * GATHER
    tiles = width // TILE
    last_m = pairs // 2 - 1

    p = lax.axis_index("ctx")
    h = lax.axis_index("ch")
    m = p // 2
    zh = p % 2
    sib_h = h + 1 - 2 * (h % 2)
    zp_h = (h + 2) % 4
    zps_h = (sib_h + 2) % 4
    sib = (p, sib_h)
    zp = (p, zp_h)
    zx = (p + 1 - 2 * zh, h)
    xm = ((p + pairs - 2) % pairs, h)
    xp = ((p + 2) % pairs, h)
    at_turn = m == last_m
    is_last = p == pairs - 1
    turned = p == pairs - 2

    loads = [
        pltpu.make_async_copy(fwd_hbm, fwd, load_sem.at[0]),
        pltpu.make_async_copy(taps_hbm, taps, load_sem.at[1]),
        pltpu.make_async_copy(back_hbm, back, load_sem.at[2]),
        pltpu.make_async_copy(gate_hbm, gate, load_sem.at[3]),
        pltpu.make_async_copy(g_hbm, gath.at[:, pl.ds(0, width)], load_sem.at[4]),
    ]
    for i, owner in enumerate((h, sib_h, zp_h, zps_h)):
        loads.append(
            pltpu.make_async_copy(
                w_hbm.at[:, pl.ds(pl.multiple_of(owner * width, width), width)],
                wbuf.at[:, pl.ds(i * width, width)],
                load_sem.at[5 + i],
            )
        )
    loads.append(pltpu.make_async_copy(starts_hbm, starts_ref, load_sem.at[9]))

    barrier = pltpu.get_barrier_semaphore()
    for peer in (sib, zp, zx, xm, xp):
        pl.semaphore_signal(barrier, inc=1, device_id=peer, device_id_type=MESH)
    for cp in loads[:2] + loads[9:]:
        cp.start()
    pl.semaphore_wait(barrier, 5)

    def ag_z(k):
        r = pl.ds(k * ra, ra)
        return pltpu.make_async_remote_copy(
            src_ref=g_hbm.at[r],
            dst_ref=gath.at[r, pl.ds(2 * width, width)],
            send_sem=ag_send.at[k],
            recv_sem=ag_recv.at[k],
            device_id=zp,
            device_id_type=MESH,
        )

    def ag_f(k):
        r = pl.ds(k * ra, ra)
        return pltpu.make_async_remote_copy(
            src_ref=gath.at[r, pl.ds(2 * width, width)],
            dst_ref=gath.at[r, pl.ds(3 * width, width)],
            send_sem=ag_send.at[n_ag + k],
            recv_sem=ag_recv.at[n_ag + k],
            device_id=sib,
            device_id_type=MESH,
        )

    ag_s = pltpu.make_async_remote_copy(
        src_ref=g_hbm,
        dst_ref=gath.at[:, pl.ds(width, width)],
        send_sem=ag_send.at[2 * n_ag],
        recv_sem=ag_recv.at[2 * n_ag],
        device_id=sib,
        device_id_type=MESH,
    )
    for k in range(n_ag):
        ag_z(k).start()
    ag_s.start()
    for cp in loads[2:9]:
        cp.start()

    def halo(kind, c, src, dst, dev, recv_kind=None):
        r = pl.ds(*PIECES[c])
        return pltpu.make_async_remote_copy(
            src_ref=slots.at[src, r],
            dst_ref=slots.at[dst, r],
            send_sem=halo_send.at[kind, c],
            recv_sem=halo_recv.at[kind if recv_kind is None else recv_kind, c],
            device_id=dev,
            device_id_type=MESH,
        )

    lz_src = jnp.where(zh == 1, OWN_L, LX)
    uz_src = jnp.where(zh == 0, OWN_U, UX)
    lf_src = jnp.where(is_last, OWN_U, LZ)
    lx_src = jnp.where(m > 0, OWN_L, UZ)

    def send_lx(c):
        return halo(S_LX, c, lx_src, LX, xm)

    def send_lz(c):
        return halo(S_LZ, c, lz_src, LZ, zx)

    def send_lf(c):
        return halo(S_LF, c, lf_src, LF, xm)

    def send_ux(c):
        return halo(S_UX, c, OWN_U, UX, xp)

    def send_uz(c):
        return halo(S_UZ, c, uz_src, UZ, zx)

    def send_uf(c):
        return halo(S_UF, c, UZ, UF, xp)

    does_lx = jnp.logical_or(m > 0, p == 0)
    does_lz = jnp.logical_or(zh == 1, m < last_m)
    has_lz = jnp.logical_or(zh == 0, m < last_m)
    does_lf = m > 0
    has_lf = m < last_m
    relays = p == 0
    does_ux = jnp.logical_or(m < last_m, is_last)
    has_ux = p > 0
    does_uf = jnp.logical_and(m < last_m, p > 0)
    has_uf = jnp.logical_and(m > 0, p > 2)

    loads[9].wait()
    starts = starts_ref[...]

    def doc_rows(base):
        pos = base + lax.broadcasted_iota(jnp.int32, (block, 128), 0)
        return jnp.sum((starts <= pos).astype(F32), axis=1, keepdims=True), pos[:, :1]

    def doc_at(pos):
        return jnp.sum((starts <= pos).astype(F32), axis=1, keepdims=True)

    def put_mask(i, cond):
        masks[i] = jnp.broadcast_to(jnp.where(cond, 1.0, 0.0), (block, TILE)).astype(BF)

    for b in range(2):
        k = p if b == 0 else 2 * pairs - 1 - p
        base = k * block
        first = doc_at(base)
        last = doc_at(base + block - 1)
        own, _ = doc_rows(base)
        put_mask(b * 6 + 0, own == last)
        put_mask(b * 6 + 4, jnp.logical_and(own == first, own != last))
        put_mask(b * 6 + 5, jnp.logical_and(own == first + 1, own != last))
        for d in range(1, 4):
            later, pos = doc_rows(base + d * block)
            put_mask(b * 6 + d, jnp.logical_and(later == last, pos < seq))

    for cp in loads[:2]:
        cp.wait()
    half = block // 2

    def taps_body(t, carry):
        cols = pl.ds(pl.multiple_of(t * TILE, TILE), TILE)
        prev = None
        for b in range(4):
            if b < 3:
                tap = taps[pl.ds(b * block, block), cols]
                high = tap.astype(BF)
                low = (tap - high.astype(F32)).astype(BF)
                spec = jnp.dot(
                    fwd[...],
                    jnp.concatenate([high, high, low], axis=0),
                    preferred_element_type=F32,
                )
                re, im = spec[:block], -spec[block:]
            else:
                re, im = None, None
            if prev is None:
                kre, kim = re, im
            else:
                pre, pim = prev
                turn_re = jnp.concatenate([pim[:half], -pim[half:]], axis=0)
                turn_im = jnp.concatenate([-pre[:half], pre[half:]], axis=0)
                if re is None:
                    kre, kim = turn_re, turn_im
                else:
                    kre, kim = re + turn_re, im + turn_im
            kern[b, pl.ds(0, block), cols] = kre
            kern[b, pl.ds(block, block), cols] = kim
            prev = (re, im)
        return carry

    lax.fori_loop(0, tiles, taps_body, 0)

    loads[4].wait()
    loads[5].wait()
    loads[6].wait()
    ag_s.wait_recv()
    nt = (((1,), (1,)), ((), ()))

    def base_body(t, carry):
        cols = pl.ds(pl.multiple_of(t * TILE, TILE), TILE)
        pacc[:, cols] = lax.dot_general(
            gath[:, pl.ds(0, 2 * width)],
            wbuf[cols, pl.ds(0, 2 * width)],
            nt,
            preferred_element_type=F32,
        )
        return carry

    lax.fori_loop(0, tiles, base_body, 0, unroll=True)

    def project(k):
        b, c = divmod(k, GATHER)
        r = pl.ds(k * ra, ra)

        def body(t, carry):
            cols = pl.ds(pl.multiple_of(t * TILE, TILE), TILE)
            part = lax.dot_general(
                gath[r, pl.ds(2 * width, 2 * width)],
                wbuf[cols, pl.ds(2 * width, 2 * width)],
                nt,
                preferred_element_type=F32,
            )
            value = (pacc[r, cols] + part) * gate[r, cols].astype(F32)
            slots[b, pl.ds(c * ra, ra), cols] = value.astype(BF)
            return carry

        lax.fori_loop(0, tiles, body, 0, unroll=True)

    def spectrum(x, mask, first=0):
        n = x.shape[0]
        xm_ = x * mask
        if n == block:
            table = fwd[:, pl.ds(0, 2 * block)]
        else:
            table = jnp.concatenate(
                [fwd[:, pl.ds(first, n)], fwd[:, pl.ds(block + first, n)]], axis=1
            )
        spec = jnp.dot(
            table, jnp.concatenate([xm_, xm_], axis=0), preferred_element_type=F32
        )
        return spec[:block], spec[block:]

    def inverse(tre, tim):
        total = jnp.concatenate([tre, tim], axis=0)
        high = total.astype(BF)
        low = (total - high.astype(F32)).astype(BF)
        return jnp.dot(
            back[...],
            jnp.concatenate([high, high, low], axis=0),
            preferred_element_type=F32,
        )

    def product(d, cols, re, im):
        kre = kern[d, pl.ds(0, block), cols]
        kim = kern[d, pl.ds(block, block), cols]
        return kre * re - kim * im, kre * im + kim * re

    def own_tile(b, t):
        cols = pl.ds(t * TILE, TILE)
        x = slots[b, :, cols]
        re, im = spectrum(x, masks[b * 6])
        tre, tim = product(0, cols, re, im)
        tot[b, pl.ds(0, block), cols] = tre
        tot[b, pl.ds(block, block), cols] = tim
        result = None
        for s in (4, 5):
            mask = masks[b * 6 + s]
            re, im = spectrum(x, mask)
            tre, tim = product(0, cols, re, im)
            part = inverse(tre, tim) * mask.astype(F32)
            result = part if result is None else result + part
        out[b, :, cols] = result

    def cross(b, d, slot, first=0, count=None):
        n = block if count is None else count
        r = pl.ds(first, n)
        for t in range(tiles):
            cols = pl.ds(t * TILE, TILE)
            re, im = spectrum(slots[slot, r, cols], masks[b * 6 + d, r], first)
            tre, tim = product(d, cols, re, im)
            tot[b, pl.ds(0, block), cols] += tre
            tot[b, pl.ds(block, block), cols] += tim

    def finish(b):
        for t in range(tiles):
            cols = pl.ds(t * TILE, TILE)
            value = inverse(tot[b, pl.ds(0, block), cols], tot[b, pl.ds(block, block), cols])
            out[b, :, cols] += value * masks[b * 6].astype(F32)

    def late(b, d, slot, first=0, count=None):
        n = block if count is None else count
        r = pl.ds(first, n)
        for t in range(tiles):
            cols = pl.ds(t * TILE, TILE)
            re, im = spectrum(slots[slot, r, cols], masks[b * 6 + d, r], first)
            tre, tim = product(d, cols, re, im)
            high = jnp.concatenate([tre, tim], axis=0).astype(BF)
            value = jnp.dot(
                back[:, pl.ds(0, 4 * block)],
                jnp.concatenate([high, high], axis=0),
                preferred_element_type=F32,
            )
            out[b, :, cols] += value * masks[b * 6].astype(F32)

    def when(cond, fn):
        pl.when(cond)(fn)

    def gather_step(k):
        ag_z(k).wait_recv()
        ag_f(k).start()
        ag_f(k).wait_recv()
        project(k)

    def pieces_of(k):
        return [c for c, (first, _) in enumerate(PIECES) if first // ra == k]

    def ux_to_uz(c):
        when(has_ux, lambda: send_ux(c).wait_recv())
        when(zh == 1, lambda: send_uz(c).start())

    def lz_to_lf(c):
        when(has_lz & (p > 0), lambda: send_lz(c).wait_recv())
        when(does_lf, lambda: send_lf(c).start())

    def uz_to_uf(c):
        send_uz(c).wait_recv()
        when(does_uf, lambda: send_uf(c).start())
        when(relays, lambda: send_lx(c).start())

    loads[3].wait()
    loads[7].wait()
    loads[8].wait()
    for k in range(GATHER):
        gather_step(k)
        for c in pieces_of(k):
            when(m > 0, lambda c=c: send_lx(c).start())
    loads[2].wait()
    for t in range(tiles):
        own_tile(0, t)

    for k in range(GATHER):
        gather_step(GATHER + k)
        for c in pieces_of(k):
            when(does_ux, lambda c=c: send_ux(c).start())
        if k == GATHER - 2:
            for c in range(CHUNKS):
                when(jnp.logical_not(at_turn), lambda c=c: send_lx(c).wait_recv())
                first = does_lz if c < 3 else does_lz & (p != 1)
                when(first, lambda c=c: send_lz(c).start())
    for c in range(CHUNKS):
        when(zh == 0, lambda c=c: send_uz(c).start())

    when(jnp.logical_not(at_turn), lambda: cross(0, 2, LX))
    ux_to_uz(0)
    ux_to_uz(1)
    lz_to_lf(0)
    own_tile(1, 0)
    lz_to_lf(1)
    own_tile(1, 1)
    ux_to_uz(2)
    lz_to_lf(2)
    own_tile(1, 2)
    ux_to_uz(3)
    ux_to_uz(4)
    for c in range(3, CHUNKS):
        when(p == 1, lambda c=c: send_lz(c).start())
    lz_to_lf(3)
    lz_to_lf(4)
    own_tile(1, 3)
    when(p > 0, lambda: cross(0, 1, jnp.where(is_last, OWN_U, LZ)))
    uz_to_uf(0)
    cross(1, 2, jnp.where(m > 0, UX, OWN_U))
    uz_to_uf(1)
    for c in range(CHUNKS):
        when(has_lf, lambda c=c: send_lf(c).wait_recv())
    cross(0, 3, jnp.where(at_turn, jnp.where(zh == 1, UX, OWN_U), LF))
    half_rows = block // 2
    uz_slot = jnp.where(p > 0, UZ, OWN_U)
    uf_slot = jnp.where(p > 2, UF, OWN_U)
    cross(1, 1, uz_slot, 0, half_rows)
    uz_to_uf(2)
    finish(0)
    uz_to_uf(3)
    uz_to_uf(4)
    cross(1, 1, uz_slot, half_rows, half_rows)
    for c in range(2):
        when(has_uf, lambda c=c: send_uf(c).wait_recv())
    cross(1, 3, uf_slot, 0, half_rows)
    finish(1)
    for c in range(2, CHUNKS):
        when(has_uf, lambda c=c: send_uf(c).wait_recv())
    late(1, 3, uf_slot, half_rows, half_rows)

    @pl.when(at_turn | relays)
    def _():
        for c in range(CHUNKS):
            when(turned, lambda c=c: send_lx(c).wait_recv())
            when(relays, lambda c=c: send_lz(c).wait_recv())
        late(
            0,
            jnp.where(relays, 1, 2),
            jnp.where(relays, LZ, jnp.where(zh == 1, UZ, LX)),
        )

    for k in range(n_ag):
        ag_z(k).wait_send()
        ag_f(k).wait_send()
    ag_s.wait_send()
    for c in range(CHUNKS):
        when(does_lx, lambda c=c: send_lx(c).wait_send())
        when(does_lz, lambda c=c: send_lz(c).wait_send())
        when(does_lf, lambda c=c: send_lf(c).wait_send())
        when(does_ux, lambda c=c: send_ux(c).wait_send())
        send_uz(c).wait_send()
        when(does_uf, lambda c=c: send_uf(c).wait_send())


def on_device(grad_out, out_weight, gate, filter_taps, doc_starts):
    pairs = lax.axis_size("ctx")
    block = grad_out.shape[2]
    width = out_weight.shape[0]
    rows = 2 * block
    features = out_weight.shape[1]
    fwd, back = dft_tables(block)
    hbm = pl.BlockSpec(memory_space=pltpu.HBM)
    call = pl.pallas_call(
        functools.partial(kernel, (pairs, block, width, 2 * pairs * block)),
        out_shape=jax.ShapeDtypeStruct((2, block, width), F32),
        in_specs=[hbm] * 7,
        out_specs=pl.BlockSpec(memory_space=pltpu.VMEM),
        scratch_shapes=[
            pltpu.VMEM((rows, features), BF),
            pltpu.VMEM((width, features), BF),
            pltpu.VMEM((rows, width), BF),
            pltpu.VMEM(filter_taps.shape, F32),
            pltpu.VMEM((1, doc_starts.shape[0]), jnp.int32),
            pltpu.VMEM(fwd.shape, BF),
            pltpu.VMEM(back.shape, BF),
            pltpu.VMEM((rows, width), F32),
            pltpu.VMEM((8, block, width), BF),
            pltpu.VMEM((4, 2 * block, width), F32),
            pltpu.VMEM((2, 2 * block, width), F32),
            pltpu.VMEM((12, block, TILE), BF),
            pltpu.SemaphoreType.DMA((10,)),
            pltpu.SemaphoreType.DMA((4 * GATHER + 1,)),
            pltpu.SemaphoreType.DMA((4 * GATHER + 1,)),
            pltpu.SemaphoreType.DMA((6, CHUNKS)),
            pltpu.SemaphoreType.DMA((6, CHUNKS)),
        ],
        compiler_params=pltpu.CompilerParams(
            collective_id=0, has_side_effects=True, vmem_limit_bytes=44 << 20
        ),
        name="gated_conv_grad",
    )
    operands = (
        grad_out.reshape(rows, width),
        out_weight,
        gate.reshape(rows, width),
        filter_taps,
        doc_starts.reshape(1, -1),
        jnp.asarray(fwd),
        jnp.asarray(back),
    )
    result = call(*[pltpu.with_memory_space_constraint(v, pltpu.HBM) for v in operands])
    return result[None]


def solution(mesh):
    in_specs = (
        P("ctx", None, None, "ch"),
        P("ch", None),
        P("ctx", None, None, "ch"),
        P(None, "ch"),
        P(),
    )
    out_specs = P("ctx", None, None, "ch")
    return jax.shard_map(
        on_device, mesh=mesh, in_specs=in_specs, out_specs=out_specs, check_vma=False
    )
```

```python
import functools
import math

import jax
import jax.numpy as jnp
import ml_dtypes
import numpy as np
from jax import lax
from jax.experimental import pallas as pl
from jax.experimental.pallas import tpu as pltpu
from jax.sharding import PartitionSpec as P

MESH = pl.DeviceIdType.MESH
BF = jnp.bfloat16
F32 = jnp.float32

GATHER = 2
PIECES = ((0, 64), (64, 64), (128, 64), (192, 32), (224, 32))
CHUNKS = len(PIECES)
TILE = 256
OWN_L, OWN_U, LX, LZ, LF, UX, UZ, UF = range(8)
S_LX, S_LZ, S_LF, S_UX, S_UZ, S_UF = range(6)


def dft_tables(block):
    order = np.concatenate([np.arange(0, block, 2), np.arange(1, block, 2)])
    omega = 2.0 * math.pi * (order + 0.5) / (2 * block)
    angle = omega[:, None] * np.arange(block)[None, :]
    forward = np.concatenate([np.cos(angle), -np.sin(angle)], axis=0)

    def parts(table):
        high = table.astype(ml_dtypes.bfloat16)
        low = (table - high.astype(np.float64)).astype(ml_dtypes.bfloat16)
        return high, low

    high, low = parts(forward)
    fwd = np.concatenate([high, low, high], axis=1)
    high, low = parts(forward.T / block)
    back = np.concatenate([high, low, high], axis=1)
    return fwd, back


def kernel(
    sizes,
    g_hbm, w_hbm, gate_hbm, taps_hbm, starts_hbm, fwd_hbm, back_hbm,
    out,
    gath, wbuf, gate, taps, starts_ref, fwd, back, pacc, slots, kern, tot, masks,
    load_sem, ag_send, ag_recv, halo_send, halo_recv,
):
    pairs, block, width, seq = sizes
    ra = block // GATHER
    n_ag = 2 * GATHER
    tiles = width // TILE
    last_m = pairs // 2 - 1

    p = lax.axis_index("ctx")
    h = lax.axis_index("ch")
    m = p // 2
    zh = p % 2
    sib_h = h + 1 - 2 * (h % 2)
    zp_h = (h + 2) % 4
    zps_h = (sib_h + 2) % 4
    sib = (p, sib_h)
    zp = (p, zp_h)
    zx = (p + 1 - 2 * zh, h)
    xm = ((p + pairs - 2) % pairs, h)
    xp = ((p + 2) % pairs, h)
    at_turn = m == last_m
    is_last = p == pairs - 1
    turned = p == pairs - 2

    loads = [
        pltpu.make_async_copy(fwd_hbm, fwd, load_sem.at[0]),
        pltpu.make_async_copy(taps_hbm, taps, load_sem.at[1]),
        pltpu.make_async_copy(back_hbm, back, load_sem.at[2]),
        pltpu.make_async_copy(gate_hbm, gate, load_sem.at[3]),
        pltpu.make_async_copy(g_hbm, gath.at[:, pl.ds(0, width)], load_sem.at[4]),
    ]
    for i, owner in enumerate((h, sib_h, zp_h, zps_h)):
        loads.append(
            pltpu.make_async_copy(
                w_hbm.at[:, pl.ds(pl.multiple_of(owner * width, width), width)],
                wbuf.at[:, pl.ds(i * width, width)],
                load_sem.at[5 + i],
            )
        )
    loads.append(pltpu.make_async_copy(starts_hbm, starts_ref, load_sem.at[9]))

    barrier = pltpu.get_barrier_semaphore()
    for peer in (sib, zp, zx, xm, xp):
        pl.semaphore_signal(barrier, inc=1, device_id=peer, device_id_type=MESH)
    for cp in loads[:2] + loads[9:]:
        cp.start()
    pl.semaphore_wait(barrier, 5)

    def ag_z(k):
        r = pl.ds(k * ra, ra)
        return pltpu.make_async_remote_copy(
            src_ref=g_hbm.at[r],
            dst_ref=gath.at[r, pl.ds(2 * width, width)],
            send_sem=ag_send.at[k],
            recv_sem=ag_recv.at[k],
            device_id=zp,
            device_id_type=MESH,
        )

    def ag_f(k):
        r = pl.ds(k * ra, ra)
        return pltpu.make_async_remote_copy(
            src_ref=gath.at[r, pl.ds(2 * width, width)],
            dst_ref=gath.at[r, pl.ds(3 * width, width)],
            send_sem=ag_send.at[n_ag + k],
            recv_sem=ag_recv.at[n_ag + k],
            device_id=sib,
            device_id_type=MESH,
        )

    ag_s = pltpu.make_async_remote_copy(
        src_ref=g_hbm,
        dst_ref=gath.at[:, pl.ds(width, width)],
        send_sem=ag_send.at[2 * n_ag],
        recv_sem=ag_recv.at[2 * n_ag],
        device_id=sib,
        device_id_type=MESH,
    )
    for k in range(n_ag):
        ag_z(k).start()
    ag_s.start()
    for cp in loads[2:9]:
        cp.start()

    def halo(kind, c, src, dst, dev, recv_kind=None):
        r = pl.ds(*PIECES[c])
        return pltpu.make_async_remote_copy(
            src_ref=slots.at[src, r],
            dst_ref=slots.at[dst, r],
            send_sem=halo_send.at[kind, c],
            recv_sem=halo_recv.at[kind if recv_kind is None else recv_kind, c],
            device_id=dev,
            device_id_type=MESH,
        )

    lz_src = jnp.where(zh == 1, OWN_L, LX)
    uz_src = jnp.where(zh == 0, OWN_U, UX)
    lf_src = jnp.where(is_last, OWN_U, LZ)
    lx_src = jnp.where(m > 0, OWN_L, UZ)

    def send_lx(c):
        return halo(S_LX, c, lx_src, LX, xm)

    def send_lz(c):
        return halo(S_LZ, c, lz_src, LZ, zx)

    def send_lf(c):
        return halo(S_LF, c, lf_src, LF, xm)

    def send_ux(c):
        return halo(S_UX, c, OWN_U, UX, xp)

    def send_uz(c):
        return halo(S_UZ, c, uz_src, UZ, zx)

    def send_uf(c):
        return halo(S_UF, c, UZ, UF, xp)

    does_lx = jnp.logical_or(m > 0, p == 0)
    does_lz = jnp.logical_or(zh == 1, m < last_m)
    has_lz = jnp.logical_or(zh == 0, m < last_m)
    does_lf = m > 0
    has_lf = m < last_m
    relays = p == 0
    does_ux = jnp.logical_or(m < last_m, is_last)
    has_ux = p > 0
    does_uf = jnp.logical_and(m < last_m, p > 0)
    has_uf = jnp.logical_and(m > 0, p > 2)

    loads[9].wait()
    starts = starts_ref[...]

    def doc_rows(base):
        pos = base + lax.broadcasted_iota(jnp.int32, (block, 128), 0)
        return jnp.sum((starts <= pos).astype(F32), axis=1, keepdims=True), pos[:, :1]

    def doc_at(pos):
        return jnp.sum((starts <= pos).astype(F32), axis=1, keepdims=True)

    def put_mask(i, cond):
        masks[i] = jnp.broadcast_to(jnp.where(cond, 1.0, 0.0), (block, TILE)).astype(BF)

    for b in range(2):
        k = p if b == 0 else 2 * pairs - 1 - p
        base = k * block
        first = doc_at(base)
        last = doc_at(base + block - 1)
        own, _ = doc_rows(base)
        put_mask(b * 6 + 0, own == last)
        put_mask(b * 6 + 4, jnp.logical_and(own == first, own != last))
        put_mask(b * 6 + 5, jnp.logical_and(own == first + 1, own != last))
        for d in range(1, 4):
            later, pos = doc_rows(base + d * block)
            put_mask(b * 6 + d, jnp.logical_and(later == last, pos < seq))

    for cp in loads[:2]:
        cp.wait()
    half = block // 2

    def taps_body(t, carry):
        cols = pl.ds(pl.multiple_of(t * TILE, TILE), TILE)
        prev = None
        for b in range(4):
            if b < 3:
                tap = taps[pl.ds(b * block, block), cols]
                high = tap.astype(BF)
                low = (tap - high.astype(F32)).astype(BF)
                spec = jnp.dot(
                    fwd[...],
                    jnp.concatenate([high, high, low], axis=0),
                    preferred_element_type=F32,
                )
                re, im = spec[:block], -spec[block:]
            else:
                re, im = None, None
            if prev is None:
                kre, kim = re, im
            else:
                pre, pim = prev
                turn_re = jnp.concatenate([pim[:half], -pim[half:]], axis=0)
                turn_im = jnp.concatenate([-pre[:half], pre[half:]], axis=0)
                if re is None:
                    kre, kim = turn_re, turn_im
                else:
                    kre, kim = re + turn_re, im + turn_im
            kern[b, pl.ds(0, block), cols] = kre
            kern[b, pl.ds(block, block), cols] = kim
            prev = (re, im)
        return carry

    lax.fori_loop(0, tiles, taps_body, 0)

    loads[4].wait()
    loads[5].wait()
    loads[6].wait()
    ag_s.wait_recv()
    nt = (((1,), (1,)), ((), ()))

    def base_body(t, carry):
        cols = pl.ds(pl.multiple_of(t * TILE, TILE), TILE)
        pacc[:, cols] = lax.dot_general(
            gath[:, pl.ds(0, 2 * width)],
            wbuf[cols, pl.ds(0, 2 * width)],
            nt,
            preferred_element_type=F32,
        )
        return carry

    lax.fori_loop(0, tiles, base_body, 0, unroll=True)

    def project(k):
        b, c = divmod(k, GATHER)
        r = pl.ds(k * ra, ra)

        def body(t, carry):
            cols = pl.ds(pl.multiple_of(t * TILE, TILE), TILE)
            part = lax.dot_general(
                gath[r, pl.ds(2 * width, 2 * width)],
                wbuf[cols, pl.ds(2 * width, 2 * width)],
                nt,
                preferred_element_type=F32,
            )
            value = (pacc[r, cols] + part) * gate[r, cols].astype(F32)
            slots[b, pl.ds(c * ra, ra), cols] = value.astype(BF)
            return carry

        lax.fori_loop(0, tiles, body, 0, unroll=True)

    def spectrum(x, mask, first=0):
        n = x.shape[0]
        xm_ = x * mask
        if n == block:
            table = fwd[:, pl.ds(0, 2 * block)]
        else:
            table = jnp.concatenate(
                [fwd[:, pl.ds(first, n)], fwd[:, pl.ds(block + first, n)]], axis=1
            )
        spec = jnp.dot(
            table, jnp.concatenate([xm_, xm_], axis=0), preferred_element_type=F32
        )
        return spec[:block], spec[block:]

    def inverse(tre, tim):
        high = jnp.concatenate([tre, tim], axis=0).astype(BF)
        return jnp.dot(
            back[:, pl.ds(0, 4 * block)],
            jnp.concatenate([high, high], axis=0),
            preferred_element_type=F32,
        )

    def product(d, cols, re, im):
        kre = kern[d, pl.ds(0, block), cols]
        kim = kern[d, pl.ds(block, block), cols]
        return kre * re - kim * im, kre * im + kim * re

    def own_tile(b, t):
        cols = pl.ds(t * TILE, TILE)
        x = slots[b, :, cols]
        re, im = spectrum(x, masks[b * 6])
        tre, tim = product(0, cols, re, im)
        tot[b, pl.ds(0, block), cols] = tre
        tot[b, pl.ds(block, block), cols] = tim
        result = None
        for s in (4, 5):
            mask = masks[b * 6 + s]
            re, im = spectrum(x, mask)
            tre, tim = product(0, cols, re, im)
            part = inverse(tre, tim) * mask.astype(F32)
            result = part if result is None else result + part
        out[b, :, cols] = result

    def cross(b, d, slot, first=0, count=None):
        n = block if count is None else count
        r = pl.ds(first, n)
        for t in range(tiles):
            cols = pl.ds(t * TILE, TILE)
            re, im = spectrum(slots[slot, r, cols], masks[b * 6 + d, r], first)
            tre, tim = product(d, cols, re, im)
            tot[b, pl.ds(0, block), cols] += tre
            tot[b, pl.ds(block, block), cols] += tim

    def finish(b):
        for t in range(tiles):
            cols = pl.ds(t * TILE, TILE)
            value = inverse(tot[b, pl.ds(0, block), cols], tot[b, pl.ds(block, block), cols])
            out[b, :, cols] += value * masks[b * 6].astype(F32)

    def late(b, d, slot, first=0, count=None):
        n = block if count is None else count
        r = pl.ds(first, n)
        for t in range(tiles):
            cols = pl.ds(t * TILE, TILE)
            re, im = spectrum(slots[slot, r, cols], masks[b * 6 + d, r], first)
            tre, tim = product(d, cols, re, im)
            high = jnp.concatenate([tre, tim], axis=0).astype(BF)
            value = jnp.dot(
                back[:, pl.ds(0, 4 * block)],
                jnp.concatenate([high, high], axis=0),
                preferred_element_type=F32,
            )
            out[b, :, cols] += value * masks[b * 6].astype(F32)

    def when(cond, fn):
        pl.when(cond)(fn)

    def gather_step(k):
        ag_z(k).wait_recv()
        ag_f(k).start()
        ag_f(k).wait_recv()
        project(k)

    def pieces_of(k):
        return [c for c, (first, _) in enumerate(PIECES) if first // ra == k]

    def ux_to_uz(c):
        when(has_ux, lambda: send_ux(c).wait_recv())
        when(zh == 1, lambda: send_uz(c).start())

    def lz_to_lf(c):
        when(has_lz & (p > 0), lambda: send_lz(c).wait_recv())
        when(does_lf, lambda: send_lf(c).start())

    def uz_to_uf(c):
        send_uz(c).wait_recv()
        when(does_uf, lambda: send_uf(c).start())
        when(relays, lambda: send_lx(c).start())

    loads[3].wait()
    loads[7].wait()
    loads[8].wait()
    for k in range(GATHER):
        gather_step(k)
        for c in pieces_of(k):
            when(m > 0, lambda c=c: send_lx(c).start())
    loads[2].wait()
    for t in range(tiles):
        own_tile(0, t)

    for k in range(GATHER):
        gather_step(GATHER + k)
        for c in pieces_of(k):
            when(does_ux, lambda c=c: send_ux(c).start())
        if k == GATHER - 2:
            for c in range(CHUNKS):
                when(jnp.logical_not(at_turn), lambda c=c: send_lx(c).wait_recv())
                first = does_lz if c < 3 else does_lz & (p != 1)
                when(first, lambda c=c: send_lz(c).start())
    for c in range(CHUNKS):
        when(zh == 0, lambda c=c: send_uz(c).start())

    when(jnp.logical_not(at_turn), lambda: cross(0, 2, LX))
    ux_to_uz(0)
    ux_to_uz(1)
    lz_to_lf(0)
    own_tile(1, 0)
    lz_to_lf(1)
    own_tile(1, 1)
    ux_to_uz(2)
    lz_to_lf(2)
    own_tile(1, 2)
    ux_to_uz(3)
    ux_to_uz(4)
    for c in range(3, CHUNKS):
        when(p == 1, lambda c=c: send_lz(c).start())
    lz_to_lf(3)
    lz_to_lf(4)
    own_tile(1, 3)
    when(p > 0, lambda: cross(0, 1, jnp.where(is_last, OWN_U, LZ)))
    uz_to_uf(0)
    cross(1, 2, jnp.where(m > 0, UX, OWN_U))
    uz_to_uf(1)
    for c in range(CHUNKS):
        when(has_lf, lambda c=c: send_lf(c).wait_recv())
    cross(0, 3, jnp.where(at_turn, jnp.where(zh == 1, UX, OWN_U), LF))
    half_rows = block // 2
    uz_slot = jnp.where(p > 0, UZ, OWN_U)
    uf_slot = jnp.where(p > 2, UF, OWN_U)
    cross(1, 1, uz_slot, 0, half_rows)
    uz_to_uf(2)
    finish(0)
    uz_to_uf(3)
    uz_to_uf(4)
    cross(1, 1, uz_slot, half_rows, half_rows)
    for c in range(2):
        when(has_uf, lambda c=c: send_uf(c).wait_recv())
    cross(1, 3, uf_slot, 0, half_rows)
    finish(1)
    for c in range(2, CHUNKS):
        when(has_uf, lambda c=c: send_uf(c).wait_recv())
    late(1, 3, uf_slot, half_rows, half_rows)

    @pl.when(at_turn | relays)
    def _():
        for c in range(CHUNKS):
            when(turned, lambda c=c: send_lx(c).wait_recv())
            when(relays, lambda c=c: send_lz(c).wait_recv())
        late(
            0,
            jnp.where(relays, 1, 2),
            jnp.where(relays, LZ, jnp.where(zh == 1, UZ, LX)),
        )

    for k in range(n_ag):
        ag_z(k).wait_send()
        ag_f(k).wait_send()
    ag_s.wait_send()
    for c in range(CHUNKS):
        when(does_lx, lambda c=c: send_lx(c).wait_send())
        when(does_lz, lambda c=c: send_lz(c).wait_send())
        when(does_lf, lambda c=c: send_lf(c).wait_send())
        when(does_ux, lambda c=c: send_ux(c).wait_send())
        send_uz(c).wait_send()
        when(does_uf, lambda c=c: send_uf(c).wait_send())


def on_device(grad_out, out_weight, gate, filter_taps, doc_starts):
    pairs = lax.axis_size("ctx")
    block = grad_out.shape[2]
    width = out_weight.shape[0]
    rows = 2 * block
    features = out_weight.shape[1]
    fwd, back = dft_tables(block)
    hbm = pl.BlockSpec(memory_space=pltpu.HBM)
    call = pl.pallas_call(
        functools.partial(kernel, (pairs, block, width, 2 * pairs * block)),
        out_shape=jax.ShapeDtypeStruct((2, block, width), F32),
        in_specs=[hbm] * 7,
        out_specs=pl.BlockSpec(memory_space=pltpu.VMEM),
        scratch_shapes=[
            pltpu.VMEM((rows, features), BF),
            pltpu.VMEM((width, features), BF),
            pltpu.VMEM((rows, width), BF),
            pltpu.VMEM(filter_taps.shape, F32),
            pltpu.VMEM((1, doc_starts.shape[0]), jnp.int32),
            pltpu.VMEM(fwd.shape, BF),
            pltpu.VMEM(back.shape, BF),
            pltpu.VMEM((rows, width), F32),
            pltpu.VMEM((8, block, width), BF),
            pltpu.VMEM((4, 2 * block, width), F32),
            pltpu.VMEM((2, 2 * block, width), F32),
            pltpu.VMEM((12, block, TILE), BF),
            pltpu.SemaphoreType.DMA((10,)),
            pltpu.SemaphoreType.DMA((4 * GATHER + 1,)),
            pltpu.SemaphoreType.DMA((4 * GATHER + 1,)),
            pltpu.SemaphoreType.DMA((6, CHUNKS)),
            pltpu.SemaphoreType.DMA((6, CHUNKS)),
        ],
        compiler_params=pltpu.CompilerParams(
            collective_id=0, has_side_effects=True, vmem_limit_bytes=44 << 20
        ),
        name="gated_conv_grad",
    )
    operands = (
        grad_out.reshape(rows, width),
        out_weight,
        gate.reshape(rows, width),
        filter_taps,
        doc_starts.reshape(1, -1),
        jnp.asarray(fwd),
        jnp.asarray(back),
    )
    result = call(*[pltpu.with_memory_space_constraint(v, pltpu.HBM) for v in operands])
    return result[None]


def solution(mesh):
    in_specs = (
        P("ctx", None, None, "ch"),
        P("ch", None),
        P("ctx", None, None, "ch"),
        P(None, "ch"),
        P(),
    )
    out_specs = P("ctx", None, None, "ch")
    return jax.shard_map(
        on_device, mesh=mesh, in_specs=in_specs, out_specs=out_specs, check_vma=False
    )
```

```python
import functools
import math

import jax
import jax.numpy as jnp
import ml_dtypes
import numpy as np
from jax import lax
from jax.experimental import pallas as pl
from jax.experimental.pallas import tpu as pltpu
from jax.sharding import PartitionSpec as P

MESH = pl.DeviceIdType.MESH
BF = jnp.bfloat16
F32 = jnp.float32

GATHER = 2
PIECES = ((0, 64), (64, 64), (128, 64), (192, 32), (224, 32))
CHUNKS = len(PIECES)
TILE = 256
OWN_L, OWN_U, LX, LZ, LF, UX, UZ, UF = range(8)
S_LX, S_LZ, S_LF, S_UX, S_UZ, S_UF = range(6)


def dft_tables(block):
    order = np.concatenate([np.arange(0, block, 2), np.arange(1, block, 2)])
    omega = 2.0 * math.pi * (order + 0.5) / (2 * block)
    angle = omega[:, None] * np.arange(block)[None, :]
    forward = np.concatenate([np.cos(angle), -np.sin(angle)], axis=0)

    def parts(table):
        high = table.astype(ml_dtypes.bfloat16)
        low = (table - high.astype(np.float64)).astype(ml_dtypes.bfloat16)
        return high, low

    high, low = parts(forward)
    fwd = np.concatenate([high, low, high], axis=1)
    high, low = parts(forward.T / block)
    back = np.concatenate([high, low, high], axis=1)
    return fwd, back


def kernel(
    sizes,
    g_hbm, w_hbm, gate_hbm, taps_hbm, starts_hbm, fwd_hbm, back_hbm,
    out,
    gath, wbuf, gate, taps, starts_ref, fwd, back, pacc, slots, kern, tot, masks,
    load_sem, ag_send, ag_recv, halo_send, halo_recv,
):
    pairs, block, width, seq = sizes
    ra = block // GATHER
    n_ag = 2 * GATHER
    tiles = width // TILE
    last_m = pairs // 2 - 1

    p = lax.axis_index("ctx")
    h = lax.axis_index("ch")
    m = p // 2
    zh = p % 2
    sib_h = h + 1 - 2 * (h % 2)
    zp_h = (h + 2) % 4
    zps_h = (sib_h + 2) % 4
    sib = (p, sib_h)
    zp = (p, zp_h)
    zx = (p + 1 - 2 * zh, h)
    xm = ((p + pairs - 2) % pairs, h)
    xp = ((p + 2) % pairs, h)
    at_turn = m == last_m
    is_last = p == pairs - 1
    turned = p == pairs - 2

    loads = [
        pltpu.make_async_copy(fwd_hbm, fwd, load_sem.at[0]),
        pltpu.make_async_copy(taps_hbm, taps, load_sem.at[1]),
        pltpu.make_async_copy(back_hbm, back, load_sem.at[2]),
        pltpu.make_async_copy(gate_hbm, gate, load_sem.at[3]),
        pltpu.make_async_copy(g_hbm, gath.at[:, pl.ds(0, width)], load_sem.at[4]),
    ]
    for i, owner in enumerate((h, sib_h, zp_h, zps_h)):
        loads.append(
            pltpu.make_async_copy(
                w_hbm.at[:, pl.ds(pl.multiple_of(owner * width, width), width)],
                wbuf.at[:, pl.ds(i * width, width)],
                load_sem.at[5 + i],
            )
        )
    loads.append(pltpu.make_async_copy(starts_hbm, starts_ref, load_sem.at[9]))

    barrier = pltpu.get_barrier_semaphore()
    for peer in (sib, zp, zx, xm, xp):
        pl.semaphore_signal(barrier, inc=1, device_id=peer, device_id_type=MESH)
    for cp in loads[:2] + loads[9:]:
        cp.start()
    pl.semaphore_wait(barrier, 5)

    def ag_z(k):
        r = pl.ds(k * ra, ra)
        return pltpu.make_async_remote_copy(
            src_ref=g_hbm.at[r],
            dst_ref=gath.at[r, pl.ds(2 * width, width)],
            send_sem=ag_send.at[k],
            recv_sem=ag_recv.at[k],
            device_id=zp,
            device_id_type=MESH,
        )

    def ag_f(k):
        r = pl.ds(k * ra, ra)
        return pltpu.make_async_remote_copy(
            src_ref=gath.at[r, pl.ds(2 * width, width)],
            dst_ref=gath.at[r, pl.ds(3 * width, width)],
            send_sem=ag_send.at[n_ag + k],
            recv_sem=ag_recv.at[n_ag + k],
            device_id=sib,
            device_id_type=MESH,
        )

    ag_s = pltpu.make_async_remote_copy(
        src_ref=g_hbm,
        dst_ref=gath.at[:, pl.ds(width, width)],
        send_sem=ag_send.at[2 * n_ag],
        recv_sem=ag_recv.at[2 * n_ag],
        device_id=sib,
        device_id_type=MESH,
    )
    for k in range(n_ag):
        ag_z(k).start()
    ag_s.start()
    for cp in loads[2:9]:
        cp.start()

    def halo(kind, c, src, dst, dev, recv_kind=None):
        r = pl.ds(*PIECES[c])
        return pltpu.make_async_remote_copy(
            src_ref=slots.at[src, r],
            dst_ref=slots.at[dst, r],
            send_sem=halo_send.at[kind, c],
            recv_sem=halo_recv.at[kind if recv_kind is None else recv_kind, c],
            device_id=dev,
            device_id_type=MESH,
        )

    lz_src = jnp.where(zh == 1, OWN_L, LX)
    uz_src = jnp.where(zh == 0, OWN_U, UX)
    lf_src = jnp.where(is_last, OWN_U, LZ)
    lx_src = jnp.where(m > 0, OWN_L, UZ)

    def send_lx(c):
        return halo(S_LX, c, lx_src, LX, xm)

    def send_lz(c):
        return halo(S_LZ, c, lz_src, LZ, zx)

    def send_lf(c):
        return halo(S_LF, c, lf_src, LF, xm)

    def send_ux(c):
        return halo(S_UX, c, OWN_U, UX, xp)

    def send_uz(c):
        return halo(S_UZ, c, uz_src, UZ, zx)

    def send_uf(c):
        return halo(S_UF, c, UZ, UF, xp)

    does_lx = jnp.logical_or(m > 0, p == 0)
    does_lz = jnp.logical_or(zh == 1, m < last_m)
    has_lz = jnp.logical_or(zh == 0, m < last_m)
    does_lf = m > 0
    has_lf = m < last_m
    relays = p == 0
    does_ux = jnp.logical_or(m < last_m, is_last)
    has_ux = p > 0
    does_uf = jnp.logical_and(m < last_m, p > 0)
    has_uf = jnp.logical_and(m > 0, p > 2)

    loads[9].wait()
    starts = starts_ref[...]

    def doc_rows(base):
        pos = base + lax.broadcasted_iota(jnp.int32, (block, 128), 0)
        return jnp.sum((starts <= pos).astype(F32), axis=1, keepdims=True), pos[:, :1]

    def doc_at(pos):
        return jnp.sum((starts <= pos).astype(F32), axis=1, keepdims=True)

    def put_mask(i, cond):
        masks[i] = jnp.broadcast_to(jnp.where(cond, 1.0, 0.0), (block, TILE)).astype(BF)

    for b in range(2):
        k = p if b == 0 else 2 * pairs - 1 - p
        base = k * block
        first = doc_at(base)
        last = doc_at(base + block - 1)
        own, _ = doc_rows(base)
        put_mask(b * 6 + 0, own == last)
        put_mask(b * 6 + 4, jnp.logical_and(own == first, own != last))
        put_mask(b * 6 + 5, jnp.logical_and(own == first + 1, own != last))
        for d in range(1, 4):
            later, pos = doc_rows(base + d * block)
            put_mask(b * 6 + d, jnp.logical_and(later == last, pos < seq))

    for cp in loads[:2]:
        cp.wait()
    half = block // 2

    def taps_body(t, carry):
        cols = pl.ds(pl.multiple_of(t * TILE, TILE), TILE)
        prev = None
        for b in range(4):
            if b < 3:
                tap = taps[pl.ds(b * block, block), cols]
                high = tap.astype(BF)
                low = (tap - high.astype(F32)).astype(BF)
                spec = jnp.dot(
                    fwd[...],
                    jnp.concatenate([high, high, low], axis=0),
                    preferred_element_type=F32,
                )
                re, im = spec[:block], -spec[block:]
            else:
                re, im = None, None
            if prev is None:
                kre, kim = re, im
            else:
                pre, pim = prev
                turn_re = jnp.concatenate([pim[:half], -pim[half:]], axis=0)
                turn_im = jnp.concatenate([-pre[:half], pre[half:]], axis=0)
                if re is None:
                    kre, kim = turn_re, turn_im
                else:
                    kre, kim = re + turn_re, im + turn_im
            kern[b, pl.ds(0, block), cols] = kre
            kern[b, pl.ds(block, block), cols] = kim
            prev = (re, im)
        return carry

    lax.fori_loop(0, tiles, taps_body, 0)

    loads[4].wait()
    loads[5].wait()
    loads[6].wait()
    ag_s.wait_recv()
    nt = (((1,), (1,)), ((), ()))

    def base_body(t, carry):
        cols = pl.ds(pl.multiple_of(t * TILE, TILE), TILE)
        pacc[:, cols] = lax.dot_general(
            gath[:, pl.ds(0, 2 * width)],
            wbuf[cols, pl.ds(0, 2 * width)],
            nt,
            preferred_element_type=F32,
        )
        return carry

    lax.fori_loop(0, tiles, base_body, 0, unroll=True)

    def near_part(k):
        r = pl.ds(k * ra, ra)
        for t in range(tiles):
            cols = pl.ds(t * TILE, TILE)
            pacc[r, cols] += lax.dot_general(
                gath[r, pl.ds(2 * width, width)],
                wbuf[cols, pl.ds(2 * width, width)],
                nt,
                preferred_element_type=F32,
            )

    def project(k):
        b, c = divmod(k, GATHER)
        r = pl.ds(k * ra, ra)

        def body(t, carry):
            cols = pl.ds(pl.multiple_of(t * TILE, TILE), TILE)
            part = lax.dot_general(
                gath[r, pl.ds(3 * width, width)],
                wbuf[cols, pl.ds(3 * width, width)],
                nt,
                preferred_element_type=F32,
            )
            value = (pacc[r, cols] + part) * gate[r, cols].astype(F32)
            slots[b, pl.ds(c * ra, ra), cols] = value.astype(BF)
            return carry

        lax.fori_loop(0, tiles, body, 0, unroll=True)

    def spectrum(x, mask, first=0):
        n = x.shape[0]
        xm_ = x * mask
        if n == block:
            table = fwd[:, pl.ds(0, 2 * block)]
        else:
            table = jnp.concatenate(
                [fwd[:, pl.ds(first, n)], fwd[:, pl.ds(block + first, n)]], axis=1
            )
        spec = jnp.dot(
            table, jnp.concatenate([xm_, xm_], axis=0), preferred_element_type=F32
        )
        return spec[:block], spec[block:]

    def inverse(tre, tim):
        high = jnp.concatenate([tre, tim], axis=0).astype(BF)
        return jnp.dot(
            back[:, pl.ds(0, 4 * block)],
            jnp.concatenate([high, high], axis=0),
            preferred_element_type=F32,
        )

    def product(d, cols, re, im):
        kre = kern[d, pl.ds(0, block), cols]
        kim = kern[d, pl.ds(block, block), cols]
        return kre * re - kim * im, kre * im + kim * re

    def own_tile(b, t):
        cols = pl.ds(t * TILE, TILE)
        x = slots[b, :, cols]
        re, im = spectrum(x, masks[b * 6])
        tre, tim = product(0, cols, re, im)
        tot[b, pl.ds(0, block), cols] = tre
        tot[b, pl.ds(block, block), cols] = tim
        result = None
        for s in (4, 5):
            mask = masks[b * 6 + s]
            re, im = spectrum(x, mask)
            tre, tim = product(0, cols, re, im)
            part = inverse(tre, tim) * mask.astype(F32)
            result = part if result is None else result + part
        out[b, :, cols] = result

    def cross(b, d, slot, first=0, count=None):
        n = block if count is None else count
        r = pl.ds(first, n)
        for t in range(tiles):
            cols = pl.ds(t * TILE, TILE)
            re, im = spectrum(slots[slot, r, cols], masks[b * 6 + d, r], first)
            tre, tim = product(d, cols, re, im)
            tot[b, pl.ds(0, block), cols] += tre
            tot[b, pl.ds(block, block), cols] += tim

    def finish(b):
        for t in range(tiles):
            cols = pl.ds(t * TILE, TILE)
            value = inverse(tot[b, pl.ds(0, block), cols], tot[b, pl.ds(block, block), cols])
            out[b, :, cols] += value * masks[b * 6].astype(F32)

    def late(b, d, slot, first=0, count=None):
        n = block if count is None else count
        r = pl.ds(first, n)
        for t in range(tiles):
            cols = pl.ds(t * TILE, TILE)
            re, im = spectrum(slots[slot, r, cols], masks[b * 6 + d, r], first)
            tre, tim = product(d, cols, re, im)
            high = jnp.concatenate([tre, tim], axis=0).astype(BF)
            value = jnp.dot(
                back[:, pl.ds(0, 2 * block)],
                high,
                preferred_element_type=F32,
            )
            out[b, :, cols] += value * masks[b * 6].astype(F32)

    def when(cond, fn):
        pl.when(cond)(fn)

    def gather_step(k):
        ag_z(k).wait_recv()
        ag_f(k).start()
        near_part(k)
        ag_f(k).wait_recv()
        project(k)

    def pieces_of(k):
        return [c for c, (first, _) in enumerate(PIECES) if first // ra == k]

    def ux_to_uz(c):
        when(has_ux, lambda: send_ux(c).wait_recv())
        when(zh == 1, lambda: send_uz(c).start())

    def lz_to_lf(c):
        when(has_lz & (p > 0), lambda: send_lz(c).wait_recv())
        when(does_lf, lambda: send_lf(c).start())

    def uz_to_uf(c):
        send_uz(c).wait_recv()
        when(does_uf, lambda: send_uf(c).start())
        when(relays, lambda: send_lx(c).start())

    loads[3].wait()
    loads[7].wait()
    loads[8].wait()
    for k in range(GATHER):
        gather_step(k)
        for c in pieces_of(k):
            when(m > 0, lambda c=c: send_lx(c).start())
    loads[2].wait()
    for t in range(tiles):
        own_tile(0, t)

    for k in range(GATHER):
        gather_step(GATHER + k)
        for c in pieces_of(k):
            when(does_ux, lambda c=c: send_ux(c).start())
        if k == GATHER - 2:
            for c in range(CHUNKS):
                when(jnp.logical_not(at_turn), lambda c=c: send_lx(c).wait_recv())
                first = does_lz if c < 3 else does_lz & (p != 1)
                when(first, lambda c=c: send_lz(c).start())
    for c in range(CHUNKS):
        when(zh == 0, lambda c=c: send_uz(c).start())

    when(jnp.logical_not(at_turn), lambda: cross(0, 2, LX))
    ux_to_uz(0)
    ux_to_uz(1)
    lz_to_lf(0)
    own_tile(1, 0)
    lz_to_lf(1)
    own_tile(1, 1)
    ux_to_uz(2)
    lz_to_lf(2)
    own_tile(1, 2)
    ux_to_uz(3)
    ux_to_uz(4)
    for c in range(3, CHUNKS):
        when(p == 1, lambda c=c: send_lz(c).start())
    lz_to_lf(3)
    lz_to_lf(4)
    own_tile(1, 3)
    when(p > 0, lambda: cross(0, 1, jnp.where(is_last, OWN_U, LZ)))
    uz_to_uf(0)
    cross(1, 2, jnp.where(m > 0, UX, OWN_U))
    uz_to_uf(1)
    for c in range(CHUNKS):
        when(has_lf, lambda c=c: send_lf(c).wait_recv())
    cross(0, 3, jnp.where(at_turn, jnp.where(zh == 1, UX, OWN_U), LF))
    half_rows = block // 2
    uz_slot = jnp.where(p > 0, UZ, OWN_U)
    uf_slot = jnp.where(p > 2, UF, OWN_U)
    cross(1, 1, uz_slot, 0, half_rows)
    uz_to_uf(2)
    finish(0)
    uz_to_uf(3)
    uz_to_uf(4)
    cross(1, 1, uz_slot, half_rows, half_rows)
    for c in range(2):
        when(has_uf, lambda c=c: send_uf(c).wait_recv())
    cross(1, 3, uf_slot, 0, half_rows)
    finish(1)
    for c in range(2, CHUNKS):
        when(has_uf, lambda c=c: send_uf(c).wait_recv())
    late(1, 3, uf_slot, half_rows, half_rows)

    @pl.when(at_turn | relays)
    def _():
        for c in range(CHUNKS):
            when(turned, lambda c=c: send_lx(c).wait_recv())
            when(relays, lambda c=c: send_lz(c).wait_recv())
        late(
            0,
            jnp.where(relays, 1, 2),
            jnp.where(relays, LZ, jnp.where(zh == 1, UZ, LX)),
        )

    for k in range(n_ag):
        ag_z(k).wait_send()
        ag_f(k).wait_send()
    ag_s.wait_send()
    for c in range(CHUNKS):
        when(does_lx, lambda c=c: send_lx(c).wait_send())
        when(does_lz, lambda c=c: send_lz(c).wait_send())
        when(does_lf, lambda c=c: send_lf(c).wait_send())
        when(does_ux, lambda c=c: send_ux(c).wait_send())
        send_uz(c).wait_send()
        when(does_uf, lambda c=c: send_uf(c).wait_send())


def on_device(grad_out, out_weight, gate, filter_taps, doc_starts):
    pairs = lax.axis_size("ctx")
    block = grad_out.shape[2]
    width = out_weight.shape[0]
    rows = 2 * block
    features = out_weight.shape[1]
    fwd, back = dft_tables(block)
    hbm = pl.BlockSpec(memory_space=pltpu.HBM)
    call = pl.pallas_call(
        functools.partial(kernel, (pairs, block, width, 2 * pairs * block)),
        out_shape=jax.ShapeDtypeStruct((2, block, width), F32),
        in_specs=[hbm] * 7,
        out_specs=pl.BlockSpec(memory_space=pltpu.VMEM),
        scratch_shapes=[
            pltpu.VMEM((rows, features), BF),
            pltpu.VMEM((width, features), BF),
            pltpu.VMEM((rows, width), BF),
            pltpu.VMEM(filter_taps.shape, F32),
            pltpu.VMEM((1, doc_starts.shape[0]), jnp.int32),
            pltpu.VMEM(fwd.shape, BF),
            pltpu.VMEM(back.shape, BF),
            pltpu.VMEM((rows, width), F32),
            pltpu.VMEM((8, block, width), BF),
            pltpu.VMEM((4, 2 * block, width), F32),
            pltpu.VMEM((2, 2 * block, width), F32),
            pltpu.VMEM((12, block, TILE), BF),
            pltpu.SemaphoreType.DMA((10,)),
            pltpu.SemaphoreType.DMA((4 * GATHER + 1,)),
            pltpu.SemaphoreType.DMA((4 * GATHER + 1,)),
            pltpu.SemaphoreType.DMA((6, CHUNKS)),
            pltpu.SemaphoreType.DMA((6, CHUNKS)),
        ],
        compiler_params=pltpu.CompilerParams(
            collective_id=0, has_side_effects=True, vmem_limit_bytes=44 << 20
        ),
        name="gated_conv_grad",
    )
    operands = (
        grad_out.reshape(rows, width),
        out_weight,
        gate.reshape(rows, width),
        filter_taps,
        doc_starts.reshape(1, -1),
        jnp.asarray(fwd),
        jnp.asarray(back),
    )
    result = call(*[pltpu.with_memory_space_constraint(v, pltpu.HBM) for v in operands])
    return result[None]


def solution(mesh):
    in_specs = (
        P("ctx", None, None, "ch"),
        P("ch", None),
        P("ctx", None, None, "ch"),
        P(None, "ch"),
        P(),
    )
    out_specs = P("ctx", None, None, "ch")
    return jax.shard_map(
        on_device, mesh=mesh, in_specs=in_specs, out_specs=out_specs, check_vma=False
    )
```
